32 devices in a mesh: groups: 2 (over y), coord: 16 (over z, x, core).
Axes of the slice: x: 2, y: 2, z: 4, core: 2. Of those that a mesh axis runs over, the one named last changes fastest.
Arguments:
- activations: bfloat16 [64, 128, 4096], P(('groups', 'coord')), parts along dimension 0, may hold values from -6 to 6
- out_grads: bfloat16 [64, 128, 4096], P(('groups', 'coord')), parts along dimension 0, may hold values from -6 to 6
- proj_in: bfloat16 [4096, 128], P('coord'), may hold values from -0.09375 to 0.09375
- proj_out: bfloat16 [4096, 128], P('coord'), may hold values from -0.09375 to 0.09375
- cov_in: float32 [128, 128], replicated
- cov_out: float32 [128, 128], replicated
- lengths: int32 [64], P(('groups', 'coord')), parts along dimension 0, may hold values from 1 to 128
- seq_ids: int32 [64], P(('groups', 'coord')), parts along dimension 0, may hold values from 0 to 31, each once
- bank: bfloat16 [1536, 16384], P(None, 'coord'), may hold values from -0.015625 to 0.015625
Outputs:
- scores: bfloat16 [64, 1536], P('groups', 'coord'), parts along dimension 0
The draws below stay inside these ranges and needn't reach their ends.
There are 2 independent parts, one for each index of `groups`. The reference program is written for one: setup_inputs(seed, part) draws one part's arguments, and reference() takes and returns one part's arrays. A program takes and returns all parts, laid end to end along the dimension named above; an argument that names none is the same for every part. Nothing has to cross between parts.
All inputs are finite; a program needn't handle non-finite values.
Results may differ from the reference program's by a relative error of at most 0.0064.
Values may be sent and summed in bfloat16 or wider, within the bound.
A program may use at most 128 MiB of HBM per device.

```python
import math
import jax
import jax.numpy as jnp
from jax import lax

D = 4096
RANK = 128
LEN = 128
SEQS = 32
QUERIES = 1536
COORDS = 16384


def make_factor(key):
    first, second = jax.random.split(key)
    mixing = jax.random.normal(first, (RANK, RANK), jnp.float32)
    lower_end, upper_end = (0.5, 5.0)
    diagonal = jnp.exp(jax.random.uniform(second, (RANK,), jnp.float32, math.log(lower_end), math.log(upper_end)))
    factor = jnp.dot(mixing, mixing.T) / RANK + jnp.diag(diagonal)
    return 0.5 * (factor + factor.T)


def draw_cov_in(key, part):
    return make_factor(jax.random.fold_in(key, 21))


def draw_cov_out(key, part):
    return make_factor(jax.random.fold_in(key, 37))


def draw_lengths(key, part):
    values = jax.random.randint(jax.random.fold_in(key, 5), (SEQS,), 1, LEN + 1)
    return values.at[0].set(LEN).at[1].set(1).astype(jnp.int32)


def strengthened(result, key, source, target, blocks, factor):
    def block_of(axis_at):
        return (jnp.arange(result.shape[axis_at]) // (result.shape[axis_at] // blocks)).reshape((-1,) + (1,) * (result.ndim - 1 - axis_at))

    one_side = jax.random.permutation(key, blocks)[block_of(target)]
    far = (block_of(target) + blocks // 2) % blocks
    return jnp.where((block_of(source) == one_side) | (block_of(source) == far), factor * result, result)


def shard_levels(stream_key, extent, shards, smallest, largest):
    factor_of, own = 1.0, jax.random.fold_in(stream_key, 6)
    for dim, parts in shards:
        steps = jnp.exp(jax.random.uniform(jax.random.fold_in(own, dim), (parts,), jnp.float32, smallest / len(shards), largest / len(shards)))
        factor_of = factor_of * jnp.repeat(steps, extent[dim] // parts).reshape([-1 if axis == dim else 1 for axis in range(len(extent))])
    return factor_of


def scatter_about(stream_key, extent, scale, bound, cuts=(), held_as=jnp.bfloat16):
    array = jax.random.normal(stream_key, extent, jnp.float32) * scale
    if len(cuts) > 0:
        array = shard_levels(stream_key, extent, cuts, -0.22, 0.18) * array
    return jnp.clip(array, min=-bound, max=bound).astype(held_as)


def heavy_noise(own_key, shape, scale, reach, cuts, heavy, held_as=jnp.bfloat16):
    values = scale * jax.random.normal(own_key, shape, jnp.float32)
    if cuts:
        values = values * shard_levels(own_key, shape, cuts, -0.22, 0.18)
    return jnp.clip(strengthened(values, jax.random.fold_in(own_key, 3), *heavy), -reach, reach).astype(held_as)


def setup_inputs(seed: int = 0, part: int = 0) -> dict:
    seeds = jax.random.split(jax.random.key(seed), 10)
    own_keys = jax.random.split(jax.random.fold_in(seeds[9], part), 10)
    activations = scatter_about(own_keys[0], (SEQS, LEN, D), 1.0, 6.0, ((0, 16),))
    out_grads = scatter_about(own_keys[1], (SEQS, LEN, D), 1.0, 6.0, ((0, 16),))
    proj_in = scatter_about(seeds[2], (D, RANK), D ** -0.5, 0.09375, ((0, 16),))
    proj_out = scatter_about(seeds[3], (D, RANK), D ** -0.5, 0.09375, ((0, 16),))
    cov_in = draw_cov_in(jax.random.fold_in(seeds[9], 71), part)
    cov_out = draw_cov_out(jax.random.fold_in(seeds[9], 71), part)
    lengths = draw_lengths(jax.random.fold_in(jax.random.fold_in(seeds[9], part), 71), part)
    seq_ids = jax.random.permutation(own_keys[7], SEQS).astype(jnp.int32)
    bank = heavy_noise(seeds[8], (QUERIES, COORDS), (COORDS * 16) ** -0.5, 0.015625, ((1, 16),), (1, 0, 16, 2.0))
    return {"activations": activations, "out_grads": out_grads, "proj_in": proj_in, "proj_out": proj_out, "cov_in": cov_in, "cov_out": cov_out, "lengths": lengths, "seq_ids": seq_ids, "bank": bank}


def inverse_factor(cov):
    size = cov.shape[0]
    damping = 0.1 * jnp.trace(cov) / size
    eye = jnp.eye(size, dtype=jnp.float32)
    lower = jnp.linalg.cholesky(cov + damping * eye)
    return jax.scipy.linalg.cho_solve((lower, True), eye)

def reference(activations, out_grads, proj_in, proj_out, cov_in, cov_out, lengths, seq_ids, bank):
    seqs, length, width = activations.shape
    rank = proj_in.shape[1]
    x_full = jnp.dot(activations.reshape(seqs * length, width).astype(jnp.float32), proj_in.astype(jnp.float32), preferred_element_type=jnp.float32).reshape(seqs, length, rank)
    position = lax.broadcasted_iota(jnp.int32, (seqs, length), 1)
    valid = (position < lengths[:, None]).astype(jnp.float32)
    x_proj = (x_full * valid[:, :, None]).astype(jnp.bfloat16)
    d_proj = jnp.dot(out_grads.reshape(seqs * length, width).astype(jnp.float32), proj_out.astype(jnp.float32), preferred_element_type=jnp.float32).reshape(seqs, length, rank).astype(jnp.bfloat16)
    grads = jnp.einsum('sto,sti->soi', d_proj.astype(jnp.float32), x_proj.astype(jnp.float32), preferred_element_type=jnp.float32)
    k_in = inverse_factor(cov_in)
    k_out = inverse_factor(cov_out)
    left = jnp.einsum('ab,sbc->sac', k_out, grads, precision=lax.Precision.HIGHEST)
    whitened = jnp.einsum('sac,cd->sad', left, k_in, precision=lax.Precision.HIGHEST)
    whitened = whitened.astype(jnp.bfloat16).reshape(seqs, rank * rank)
    raw = lax.dot_general(whitened.astype(jnp.float32), bank.astype(jnp.float32), (((1,), (1,)), ((), ())), preferred_element_type=jnp.float32).astype(jnp.bfloat16)
    return jnp.zeros_like(raw).at[seq_ids].set(raw)
```

```python
import functools

import jax
import jax.numpy as jnp
from jax import lax
from jax.experimental import pallas as pl
from jax.experimental.pallas import tpu as pltpu
from jax.sharding import PartitionSpec as P

MESH = pl.DeviceIdType.MESH
F32 = jnp.float32
BF16 = jnp.bfloat16
PANEL = 8
PARTS = 1
EARLY = 1
HEAD = 8
STRIDE = 2


def xor(value, mask):
    bit = 1
    result = value
    while bit <= mask:
        if mask & bit:
            result = result + bit - 2 * bit * ((value // bit) % 2)
        bit *= 2
    return result


def start_factor(cov):
    size = cov.shape[0]
    rows = lax.broadcasted_iota(jnp.int32, (size, size), 0)
    lanes = lax.broadcasted_iota(jnp.int32, (size, size), 1)
    diagonal = jnp.where(rows == lanes, cov, 0.0)
    damping = 0.1 * jnp.sum(diagonal) / size
    return jnp.where(rows == lanes, cov + damping, cov)


def eliminate_panel(matrix):
    size = matrix.shape[0]
    top, rest = matrix[:PANEL], matrix[PANEL:]
    lane = lax.broadcasted_iota(jnp.int32, (PANEL, size), 1)
    sub = lax.broadcasted_iota(jnp.int32, (PANEL, size), 0)
    pivots = [jnp.broadcast_to(top[:, r : r + 1], (PANEL, size)) for r in range(PANEL)]
    top = jnp.where(lane < PANEL, jnp.where(lane == sub, 1.0, 0.0), top)
    for r in range(PANEL):
        factor = pivots[r]
        inverse = 1.0 / factor[r : r + 1]

        def reduced(value):
            scaled = value[r : r + 1] * inverse
            return jnp.where(sub == r, scaled, value - factor * scaled)

        top = reduced(top)
        for later in range(r + 1, PANEL):
            pivots[later] = reduced(pivots[later])
    column = rest
    rest = jnp.where(lane[:1] < PANEL, 0.0, rest)
    for r in range(PANEL):
        rest = rest - column[:, r : r + 1] * top[r : r + 1]
    whole = jnp.concatenate([rest, top], axis=0)
    return pltpu.roll(whole, size - PANEL, 1)


def split(value):
    high = value.astype(BF16)
    return high, (value - high.astype(F32)).astype(BF16)


def kernel(
    n, slow, fast,
    act_ref, og_ref, pin_ref, pout_ref, cin_ref, cout_ref, len_hbm, ids_hbm, bank_ref,
    out_ref, len_ref, ids_ref,
    x, proj, w, stage, bank, factor, halves, mine_buf, theirs_buf, idbuf, wide_white, wsend, wrecv, white, psend, precv,
    load_sem, gs_sem, gr_sem, relay_sem, pair_send, pair_recv, is_sem, ir_sem, ws_sem, wr_sem, ps_sem, pr_sem,
):
    group = lax.axis_index("groups")
    me = lax.axis_index("coord")
    core = me % 2
    seqs = len_ref.shape[0]
    length = x.shape[1] // seqs
    rank = cin_ref.shape[0]
    shard = pin_ref.shape[0]
    queries = out_ref.shape[1]
    per = bank_ref.shape[1] // rank
    block = wsend.shape[1]
    level = me // (2 * fast)
    forwards = core == group

    def both(first, second):
        pl.when(core == 0)(first)
        pl.when(core == 1)(second)

    def load(src, dst, at):
        return pltpu.make_async_copy(src, dst, load_sem.at[at])

    own_w = [load(pin_ref, w.at[me], 0), load(pout_ref, w.at[me], 0)]
    own_s = [load(pout_ref, stage, 1), load(pin_ref, stage, 1)]
    own_f = [load(cin_ref, factor, 2), load(cout_ref, factor, 2)]
    own_x = [load(act_ref, x.at[core], 3), load(og_ref, x.at[core], 3)]
    for pair in (own_w, own_s, own_f):
        both(pair[0].start, pair[1].start)
    len_load, ids_load = load(len_hbm, len_ref, 4), load(ids_hbm, ids_ref, 5)
    bank_load = load(bank_ref, bank.at[pl.ds(0, bank_ref.shape[0])], 6)
    len_load.start()
    ids_load.start()

    fasts = [2 * b for b in range(1, fast)]
    slows = [2 * fast * a for a in range(1, slow)]
    early = slows[:EARLY]
    twin = (1 - group, me)

    def peer(mask):
        return (group, xor(me, mask))

    barrier = pltpu.get_barrier_semaphore()

    def signal(semaphore, to):
        pl.semaphore_signal(semaphore, inc=1, device_id=to, device_id_type=MESH)

    below, above = (group, me - 2 * fast), (group, me + 2 * fast)
    has_below, has_above = level > 0, level < slow - 1
    pl.when(has_below)(lambda: signal(barrier, below))
    pl.when(has_above)(lambda: signal(barrier, above))
    signal(barrier, twin)
    for mask in fasts + [1]:
        signal(barrier, peer(mask))
    both(own_x[0].start, own_x[1].start)
    bank_load.start()

    own_w[0].wait()
    own_s[0].wait()
    pl.semaphore_wait(barrier, 1 + fast + jnp.minimum(level, 1) + jnp.minimum(slow - 1 - level, 1))

    piece = shard // PARTS
    count = [0]
    all_sends, forward_sends = [], []

    def shard_copy(slot, part, to, at, src=None):
        rows = pl.ds(part * piece, piece)
        return pltpu.make_async_remote_copy(
            src_ref=w.at[slot, rows] if src is None else src.at[rows], dst_ref=w.at[slot, rows],
            send_sem=gs_sem.at[at], recv_sem=gr_sem.at[slot, part],
            device_id=to, device_id_type=MESH,
        )

    def send(mask, part, to, sink, src=None):
        at = count[0]

        def make():
            device = (1 - group, xor(me, to[1])) if to[0] else (group, xor(me, to[1]))
            return shard_copy(xor(me, mask), part, device, at, src)

        count[0] += 1
        make().start()
        sink.append(make)

    def arrived(mask):
        for part in range(PARTS):
            shard_copy(xor(me, mask), part, peer(1), 0).wait_recv()

    def pair_copy(src, dst, at):
        return pltpu.make_async_remote_copy(
            src_ref=src, dst_ref=dst, send_sem=pair_send.at[at], recv_sem=pair_recv.at[at],
            device_id=peer(1), device_id_type=MESH,
        )

    def along(masks, sources):
        @pl.when(forwards)
        def _():
            for source in sources:
                for part in range(PARTS):
                    for mask in masks:
                        send(source, part, (0, mask), forward_sends)

    def relay(step):
        @pl.when(forwards)
        def _():
            pl.when(has_below)(lambda: signal(relay_sem.at[step, 0], below))
            pl.when(has_above)(lambda: signal(relay_sem.at[step, 1], above))

    def relayed(step):
        @pl.when(forwards)
        def _():
            pl.when(has_above)(lambda: pl.semaphore_wait(relay_sem.at[step, 0], 1))
            pl.when(has_below)(lambda: pl.semaphore_wait(relay_sem.at[step, 1], 1))

    for part in range(PARTS):
        send(0, part, (0, 1), all_sends, stage)
    if slow > 2:
        relay(1)
    along(slows[:1], [0])
    for part in range(PARTS):
        for mask in fasts:
            send(0, part, (0, mask), all_sends)
    x_pair = [pair_copy(og_ref, x.at[core], 0), pair_copy(act_ref, x.at[core], 0)]
    both(x_pair[0].start, x_pair[1].start)
    own_f[0].wait()
    factor[...] = start_factor(factor[...])

    panels = rank // PANEL

    def step(_, carry):
        factor[...] = eliminate_panel(factor[...])
        return carry

    done = [0]

    def advance(upto):
        upto = min(upto, panels)
        if upto > done[0]:
            lax.fori_loop(0, upto - done[0], step, 0)
            done[0] = upto

    arrived(1)
    along(slows[:1], [1])
    for part in range(PARTS):
        for mask in fasts:
            send(1, part, (0, mask), all_sends)
    for at in range(1, slow - 1):
        relayed(at)
        if at + 1 < slow - 1:
            relay(at + 1)
        along(slows[at : at + 1], [0, 1])

    len_load.wait()
    ids_load.wait()
    for s in range(seqs):
        idbuf[me, s : s + 1] = jnp.full((1, idbuf.shape[2]), ids_ref[s], jnp.int32)
    tail = bank.shape[0] - bank_ref.shape[0]
    if tail:
        bank[bank_ref.shape[0] :] = jnp.zeros((tail, bank.shape[1]), BF16)
    if block > seqs * per:
        wide_white[...] = jnp.zeros_like(wide_white)
    advance(HEAD)

    known, id_copies = [], []

    def send_ids():
        for j in known:
            copy = pltpu.make_async_remote_copy(
                src_ref=idbuf.at[me], dst_ref=idbuf.at[me],
                send_sem=is_sem.at[j], recv_sem=ir_sem.at[j],
                device_id=peer(j), device_id_type=MESH,
            )
            copy.start()
            id_copies.append(copy)
        known.clear()

    def from_near():
        for b in fasts:
            for c in range(2):
                arrived(b + c)
                known.append(b + c)
        known.append(1)

    def from_slow(mask):
        for c in range(2):
            for part in range(PARTS):
                shard_copy(xor(me, mask + c), part, peer(1), 0).wait_recv()

                @pl.when(forwards)
                def _():
                    for b in fasts:
                        send(mask + c, part, (0, b), forward_sends)
                    send(mask + c, part, (1, 0), forward_sends)
                    if mask not in early:
                        for b in fasts:
                            send(mask + c, part, (1, b), forward_sends)

            known.append(mask + c)

    def from_fast(mask):
        for b in fasts:
            for c in range(2):
                arrived(mask + b + c)
                if mask in early:

                    @pl.when(forwards)
                    def _():
                        for part in range(PARTS):
                            send(mask + b + c, part, (1, 0), forward_sends)

                known.append(mask + b + c)

    span = n // slow * shard

    def add(first, slots, shards, columns):
        value = jnp.dot(
            x[:, :, columns].reshape(2 * seqs * length, -1), w[shards].reshape(slots * shard, rank),
            preferred_element_type=F32,
        ).reshape(2, seqs * length, rank)
        if first:
            proj[...] = value
        else:
            proj[...] += value

    def project(mask):
        if mask == 0:
            own_x[0].wait()
            x_pair[0].wait_recv()
        at = xor(level, mask // (2 * fast))
        add(mask == 0, 2 * fast, pl.ds(at * 2 * fast, 2 * fast), pl.ds(pl.multiple_of(at * span, 128), span))

    events = [from_near]
    for at, mask in enumerate(slows):
        events.append(functools.partial(from_slow, mask))
        if at:
            events.append(functools.partial(from_fast, slows[at - 1]))
        events.append(functools.partial(project, slows[at - 1] if at else 0))
    if slows:
        events.append(functools.partial(from_fast, slows[-1]))
        events.append(functools.partial(project, slows[-1]))
    else:
        events.append(functools.partial(project, 0))

    sent_factor = []

    def finish_factor():
        high, low = split(factor[...])
        halves[core, 0] = high
        halves[core, 1] = low
        copy = pair_copy(halves.at[core], halves.at[core], 1)
        copy.start()
        sent_factor.append(copy)

    upto = HEAD
    for at, event in enumerate(events):
        event()
        if at < len(events) - 1:
            send_ids()
            upto += STRIDE
            advance(upto if at < len(events) - 4 else panels)
            if done[0] == panels and not sent_factor:
                finish_factor()
    if not sent_factor:
        advance(panels)
        finish_factor()

    theirs_buf_send = mine_buf.at[1]
    mine_buf[1] = proj[1 - core].astype(BF16)
    swap = pair_copy(theirs_buf_send, theirs_buf, 2)
    swap.start()
    send_ids()
    mine = proj[core].astype(BF16)
    sent_factor[0].wait_recv()
    swap.wait_recv()
    theirs = theirs_buf[...]
    x_proj = jnp.where(core == 0, mine, theirs)
    d_proj = jnp.where(core == 0, theirs, mine)

    position = lax.broadcasted_iota(jnp.int32, (length, 1), 0)
    grads = []
    for s in range(seqs):
        rows = slice(s * length, (s + 1) * length)
        valid = (position < len_ref[s]).astype(BF16)
        grads.append(
            lax.dot_general(
                d_proj[rows], x_proj[rows] * valid, (((0,), (0,)), ((), ())), preferred_element_type=F32
            )
        )
    high, low = split(jnp.concatenate(grads, axis=1))
    left = jnp.dot(
        jnp.concatenate([halves[1, 0], halves[1, 0], halves[1, 1]], axis=1),
        jnp.concatenate([high, low, high], axis=0),
        preferred_element_type=F32,
    )
    high, low = split(jnp.concatenate([left[:, s * rank : (s + 1) * rank] for s in range(seqs)], axis=0))
    whites = jnp.dot(
        jnp.concatenate([high, low, high], axis=1),
        jnp.concatenate([halves[0, 0], halves[0, 0], halves[0, 1]], axis=0),
        preferred_element_type=F32,
    ).reshape(seqs, n, per, rank)
    if per % 8 == 0 and block == seqs * per:
        wsend[...] = jnp.concatenate([whites[s] for s in range(seqs)], axis=1).astype(BF16)
    else:
        for s in range(seqs):
            wide_white[:, s * per : (s + 1) * per] = whites[s]
        wsend[...] = wide_white[...].astype(BF16)

    def exchange(src, dst, send_sem, recv_sem, j):
        copy = pltpu.make_async_remote_copy(
            src_ref=src, dst_ref=dst,
            send_sem=send_sem.at[j], recv_sem=recv_sem.at[j],
            device_id=peer(j), device_id_type=MESH,
        )
        copy.start()
        return copy

    white_copies = [
        exchange(wsend.at[xor(me, j)], wrecv.at[me], ws_sem, wr_sem, j) for j in range(n - 1, 0, -1)
    ]
    wrecv[me] = wsend[me]
    bank_load.wait()
    for copy in white_copies:
        copy.wait_recv()
    white[...] = wrecv[...].astype(F32).reshape(n * block, rank)

    columns = jnp.concatenate(
        [
            jnp.concatenate(
                [white[pl.ds(s * per + a, n, stride=block), :] for s in range(seqs)], axis=0
            ).astype(BF16)
            for a in range(per)
        ],
        axis=1,
    )

    def partial(target):
        rows = bank[pl.ds(pl.multiple_of(target * queries, queries), psend.shape[2])]
        return lax.dot_general(columns, rows, (((1,), (1,)), ((), ())), preferred_element_type=F32)

    score_copies = []
    for j in range(n - 1, 0, -1):
        psend[j] = partial(xor(me, j)).astype(BF16)
        score_copies.append(exchange(psend.at[j], precv.at[j], ps_sem, pr_sem, j))
    total = partial(me)
    for copy in id_copies:
        copy.wait_recv()
    ids = jnp.concatenate([idbuf[:, s, :] for s in range(seqs)], axis=0)[:, :1]
    held = n * seqs
    one_hot = (ids == lax.broadcasted_iota(jnp.int32, (held, held), 1)).astype(BF16)
    for make in all_sends:
        make().wait_send()

    @pl.when(forwards)
    def _():
        for make in forward_sends:
            make().wait_send()

    for copy in [x_pair[0], swap] + sent_factor + id_copies + white_copies:
        copy.wait_send()
    for copy in score_copies:
        copy.wait_recv()
    for j in range(n - 1, 0, -1):
        total += precv[j].astype(F32)
    placed = lax.dot_general(
        one_hot, total.astype(BF16), (((0,), (0,)), ((), ())), preferred_element_type=F32
    )
    out_ref[...] = placed[:, :queries].astype(BF16)
    for copy in score_copies:
        copy.wait_send()


def solution(mesh):
    n = mesh.shape["coord"]
    assert mesh.shape["groups"] == 2
    chips = n // 2
    slow = 1
    while slow * slow < chips:
        slow *= 2
    fast = chips // slow

    def body(activations, out_grads, proj_in, proj_out, cov_in, cov_out, lengths, seq_ids, bank):
        seqs, length, width = activations.shape
        shard, rank = proj_in.shape
        per = bank.shape[1] // rank
        queries = bank.shape[0] // n
        wide = -(-queries // 128) * 128
        block = -(-(seqs * per) // 16) * 16
        held = n * seqs
        sends = 2 * (1 + fast) + 2 * slow + 2 * (slow - 1) * 2 * fast + 2 * slow * fast
        vmem = pl.BlockSpec(memory_space=pltpu.VMEM)
        hbm = pl.BlockSpec(memory_space=pltpu.HBM)
        dma = pltpu.SemaphoreType.DMA
        return pl.pallas_call(
            functools.partial(kernel, n, slow, fast),
            out_shape=jax.ShapeDtypeStruct((held, queries), BF16),
            in_specs=[hbm] * 9,
            out_specs=vmem,
            scratch_shapes=[
                pltpu.SMEM((seqs,), jnp.int32),
                pltpu.SMEM((seqs,), jnp.int32),
                pltpu.VMEM((2, seqs * length, width), BF16),
                pltpu.VMEM((2, seqs * length, rank), F32),
                pltpu.VMEM((n, shard, rank), BF16),
                pltpu.VMEM((shard, rank), BF16),
                pltpu.VMEM((bank.shape[0] + wide - queries, bank.shape[1]), BF16),
                pltpu.VMEM((rank, rank), F32),
                pltpu.VMEM((2, 2, rank, rank), BF16),
                pltpu.VMEM((2, seqs * length, rank), BF16),
                pltpu.VMEM((seqs * length, rank), BF16),
                pltpu.VMEM((n, seqs, 128), jnp.int32),
                pltpu.VMEM((n, block, rank), F32),
                pltpu.VMEM((n, block, rank), BF16),
                pltpu.VMEM((n, block, rank), BF16),
                pltpu.VMEM((n * block, rank), F32),
                pltpu.VMEM((n, held, wide), BF16),
                pltpu.VMEM((n, held, wide), BF16),
                dma((7,)),
                dma((sends * PARTS,)), dma((n, PARTS)), pltpu.SemaphoreType.REGULAR((max(slow, 2), 2)),
                dma((3,)), dma((3,)), dma((n,)), dma((n,)),
                dma((n,)), dma((n,)), dma((n,)), dma((n,)),
            ],
            compiler_params=pltpu.CompilerParams(
                collective_id=0, has_side_effects=True, vmem_limit_bytes=60 * 2**20
            ),
        )(
            activations.reshape(seqs * length, width), out_grads.reshape(seqs * length, width),
            proj_in, proj_out, cov_in, cov_out, lengths, seq_ids, bank,
        )

    in_specs = (
        P(("groups", "coord"), None, None),
        P(("groups", "coord"), None, None),
        P("coord", None),
        P("coord", None),
        P(),
        P(),
        P(("groups", "coord")),
        P(("groups", "coord")),
        P(None, "coord"),
    )
    return jax.shard_map(body, mesh=mesh, in_specs=in_specs, out_specs=P("groups", "coord"), check_vma=False)
```

```python
import functools

import jax
import jax.numpy as jnp
from jax import lax
from jax.experimental import pallas as pl
from jax.experimental.pallas import tpu as pltpu
from jax.sharding import PartitionSpec as P

MESH = pl.DeviceIdType.MESH
F32 = jnp.float32
BF16 = jnp.bfloat16
PANEL = 8
PARTS = 1
EARLY = 3


def xor(value, mask):
    bit = 1
    result = value
    while bit <= mask:
        if mask & bit:
            result = result + bit - 2 * bit * ((value // bit) % 2)
        bit *= 2
    return result


def start_factor(cov):
    size = cov.shape[0]
    rows = lax.broadcasted_iota(jnp.int32, (size, size), 0)
    lanes = lax.broadcasted_iota(jnp.int32, (size, size), 1)
    diagonal = jnp.where(rows == lanes, cov, 0.0)
    damping = 0.1 * jnp.sum(diagonal) / size
    return jnp.where(rows == lanes, cov + damping, cov)


def eliminate_panel(matrix):
    size = matrix.shape[0]
    top, rest = matrix[:PANEL], matrix[PANEL:]
    lane = lax.broadcasted_iota(jnp.int32, (PANEL, size), 1)
    sub = lax.broadcasted_iota(jnp.int32, (PANEL, size), 0)
    pivots = [jnp.broadcast_to(top[:, r : r + 1], (PANEL, size)) for r in range(PANEL)]
    top = jnp.where(lane < PANEL, jnp.where(lane == sub, 1.0, 0.0), top)
    for r in range(PANEL):
        factor = pivots[r]
        inverse = 1.0 / factor[r : r + 1]

        def reduced(value):
            scaled = value[r : r + 1] * inverse
            return jnp.where(sub == r, scaled, value - factor * scaled)

        top = reduced(top)
        for later in range(r + 1, PANEL):
            pivots[later] = reduced(pivots[later])
    column = rest
    rest = jnp.where(lane[:1] < PANEL, 0.0, rest)
    for r in range(PANEL):
        rest = rest - column[:, r : r + 1] * top[r : r + 1]
    whole = jnp.concatenate([rest, top], axis=0)
    return pltpu.roll(whole, size - PANEL, 1)


def split(value):
    high = value.astype(BF16)
    return high, (value - high.astype(F32)).astype(BF16)


def kernel(
    n, slow, fast,
    act_ref, og_ref, pin_ref, pout_ref, cin_ref, cout_ref, len_hbm, ids_hbm, bank_ref,
    out_ref, len_ref, ids_ref,
    x, proj, w, stage, bank, factor, halves, mine_buf, theirs_buf, idbuf, wide_white, wsend, wrecv, white, psend, precv,
    load_sem, gs_sem, gr_sem, relay_sem, pair_send, pair_recv, is_sem, ir_sem, ws_sem, wr_sem, ps_sem, pr_sem,
):
    group = lax.axis_index("groups")
    me = lax.axis_index("coord")
    core = me % 2
    seqs = len_ref.shape[0]
    length = x.shape[1] // seqs
    rank = cin_ref.shape[0]
    shard = pin_ref.shape[0]
    queries = out_ref.shape[1]
    per = bank_ref.shape[1] // rank
    block = wsend.shape[1]
    level = me // (2 * fast)
    forwards = core == group

    def both(first, second):
        pl.when(core == 0)(first)
        pl.when(core == 1)(second)

    def load(src, dst, at):
        return pltpu.make_async_copy(src, dst, load_sem.at[at])

    own_w = [load(pin_ref, w.at[me], 0), load(pout_ref, w.at[me], 0)]
    own_s = [load(pout_ref, stage, 1), load(pin_ref, stage, 1)]
    own_f = [load(cin_ref, factor.at[0], 2), load(cout_ref, factor.at[1], 7)]
    own_x = [load(act_ref, x.at[core], 3), load(og_ref, x.at[core], 3)]
    for pair in (own_w, own_s):
        both(pair[0].start, pair[1].start)
    own_f[0].start()
    own_f[1].start()
    len_load, ids_load = load(len_hbm, len_ref, 4), load(ids_hbm, ids_ref, 5)
    bank_load = load(bank_ref, bank.at[pl.ds(0, bank_ref.shape[0])], 6)
    len_load.start()
    ids_load.start()

    fasts = [2 * b for b in range(1, fast)]
    ranks = range(1, slow)
    early = ranks[:EARLY]
    twin = (1 - group, me)
    chip = 2 * fast
    near = [xor(me, chip * a) for a in range(slow)]
    inner = jnp.minimum(level, 1) * jnp.minimum(slow - 1 - level, 1)
    if slow == 4:
        near[2:] = [near[2] + inner * (near[3] - near[2]), near[3] + inner * (near[2] - near[3])]

    def slot(rank_at, off):
        return xor(near[rank_at], off)

    def peer(mask):
        return (group, xor(me, mask))

    barrier = pltpu.get_barrier_semaphore()

    def signal(semaphore, to):
        pl.semaphore_signal(semaphore, inc=1, device_id=to, device_id_type=MESH)

    below, above = (group, me - 2 * fast), (group, me + 2 * fast)
    has_below, has_above = level > 0, level < slow - 1
    pl.when(has_below)(lambda: signal(barrier, below))
    pl.when(has_above)(lambda: signal(barrier, above))
    signal(barrier, twin)
    for mask in fasts + [1]:
        signal(barrier, peer(mask))
    both(own_x[0].start, own_x[1].start)
    bank_load.start()

    own_w[0].wait()
    own_s[0].wait()
    pl.semaphore_wait(barrier, 1 + fast + jnp.minimum(level, 1) + jnp.minimum(slow - 1 - level, 1))

    piece = shard // PARTS
    count = [0]
    all_sends, forward_sends = [], []

    def shard_copy(place, part, to, at, src=None):
        rows = pl.ds(part * piece, piece)
        return pltpu.make_async_remote_copy(
            src_ref=w.at[place, rows] if src is None else src.at[rows], dst_ref=w.at[place, rows],
            send_sem=gs_sem.at[at], recv_sem=gr_sem.at[place, part],
            device_id=to, device_id_type=MESH,
        )

    def send(source, part, to, sink, src=None):
        at = count[0]

        def make():
            device = (1 - group if to[0] else group, slot(to[1], to[2]))
            return shard_copy(slot(*source), part, device, at, src)

        count[0] += 1
        make().start()
        sink.append(make)

    def arrived(rank_at, off, parts=range(PARTS)):
        for part in parts:
            shard_copy(slot(rank_at, off), part, peer(1), 0).wait_recv()

    def pair_copy(src, dst, at):
        return pltpu.make_async_remote_copy(
            src_ref=src, dst_ref=dst, send_sem=pair_send.at[at], recv_sem=pair_recv.at[at],
            device_id=peer(1), device_id_type=MESH,
        )

    def along(rank_at, sources, which):
        group_of = []

        @pl.when(which)
        def _():
            for source in sources:
                for part in range(PARTS):
                    send((0, source), part, (0, rank_at, 0), group_of)

        forward_sends.append((which, group_of))

    def relay(step):
        @pl.when(forwards)
        def _():
            pl.when(has_below)(lambda: signal(relay_sem.at[step, 0], below))
            pl.when(has_above)(lambda: signal(relay_sem.at[step, 1], above))

    def relayed(step):
        @pl.when(forwards)
        def _():
            pl.when(has_above)(lambda: pl.semaphore_wait(relay_sem.at[step, 0], 1))
            pl.when(has_below)(lambda: pl.semaphore_wait(relay_sem.at[step, 1], 1))

    for part in range(PARTS):
        send((0, 0), part, (0, 0, 1), all_sends, stage)
    if slow > 2:
        relay(1)
    middle = jnp.logical_and(forwards, inner == 1)
    outer = jnp.logical_and(forwards, inner == 0)
    special = slow == 4
    if slow > 1:
        along(1, [0], forwards)
    if special:
        along(2, [0], middle)
    for part in range(PARTS):
        for mask in fasts:
            send((0, 0), part, (0, 0, mask), all_sends)
    x_pair = [pair_copy(og_ref, x.at[core], 0), pair_copy(act_ref, x.at[core], 0)]
    both(x_pair[0].start, x_pair[1].start)
    own_f[0].wait()
    own_f[1].wait()

    def step(_, carry):
        first, second = factor[0], factor[1]
        factor[0] = eliminate_panel(first)
        factor[1] = eliminate_panel(second)
        return carry

    def factor_copy():
        return pair_copy(halves, halves, 1)

    arrived(0, 1)
    if slow > 1:
        along(1, [1], forwards)
    if special:
        along(2, [1], middle)
    for part in range(PARTS):
        for mask in fasts:
            send((0, 1), part, (0, 0, mask), all_sends)
    for at in range(1, slow - 1):
        relayed(at)
        if at + 1 < slow - 1:
            relay(at + 1)
        if not special:
            along(at + 1, [0, 1], forwards)
        elif at == 1:
            along(3, [0, 1], middle)
            along(2, [0, 1], outer)
        else:
            along(3, [0, 1], outer)

    len_load.wait()
    ids_load.wait()
    for s in range(seqs):
        idbuf[me, s : s + 1] = jnp.full((1, idbuf.shape[2]), ids_ref[s], jnp.int32)
    tail = bank.shape[0] - bank_ref.shape[0]
    if tail:
        bank[bank_ref.shape[0] :] = jnp.zeros((tail, bank.shape[1]), BF16)
    if block > seqs * per:
        wide_white[...] = jnp.zeros_like(wide_white)

    @pl.when(jnp.logical_not(forwards))
    def _():
        for at in range(2):
            factor[at] = start_factor(factor[at])
        lax.fori_loop(0, rank // PANEL, step, 0)
        for at in range(2):
            high, low = split(factor[at])
            halves[at, 0] = high
            halves[at, 1] = low
        factor_copy().start()

    known = []

    def id_copy(place, to):
        return pltpu.make_async_remote_copy(
            src_ref=idbuf.at[place], dst_ref=idbuf.at[place],
            send_sem=is_sem.at[to], recv_sem=ir_sem.at[place],
            device_id=(group, to), device_id_type=MESH,
        )

    def send_ids():
        for source in known:
            id_copy(me, slot(*source)).start()
        known.clear()

    def from_near():
        for b in fasts:
            for c in range(2):
                arrived(0, b + c)
                known.append((0, b + c))
        known.append((0, 1))

    def from_slow(rank_at):
        for c in range(2):
            for part in range(PARTS):
                arrived(rank_at, c, [part])
                group_of = []

                @pl.when(forwards)
                def _():
                    source = (rank_at, c)
                    for b in fasts:
                        send(source, part, (0, 0, b), group_of)
                    send(source, part, (1, 0, 0), group_of)
                    if rank_at not in early:
                        for b in fasts:
                            send(source, part, (1, 0, b), group_of)

                forward_sends.append((forwards, group_of))
            known.append((rank_at, c))

    def from_fast(rank_at):
        for b in fasts:
            for c in range(2):
                for part in range(PARTS):
                    arrived(rank_at, b + c, [part])
                    if rank_at in early:
                        group_of = []

                        @pl.when(forwards)
                        def _():
                            send((rank_at, b + c), part, (1, 0, 0), group_of)

                        forward_sends.append((forwards, group_of))
                known.append((rank_at, b + c))

    span = n // slow * shard

    def add(first, slots, shards, columns):
        value = jnp.dot(
            x[:, :, columns].reshape(2 * seqs * length, -1), w[shards].reshape(slots * shard, rank),
            preferred_element_type=F32,
        ).reshape(2, seqs * length, rank)
        if first:
            proj[...] = value
        else:
            proj[...] += value

    def project(rank_at):
        if rank_at == 0:
            own_x[0].wait()
            x_pair[0].wait_recv()
        at = near[rank_at] // chip
        add(rank_at == 0, chip, pl.ds(at * chip, chip), pl.ds(pl.multiple_of(at * span, 128), span))

    events = [from_near]
    for at in ranks:
        events.append(functools.partial(from_slow, at))
        if at > 1:
            events.append(functools.partial(from_fast, at - 1))
        events.append(functools.partial(project, at - 1))
    if slow > 1:
        events.append(functools.partial(from_fast, slow - 1))
    events.append(functools.partial(project, slow - 1))

    for at, event in enumerate(events):
        event()
        if at < len(events) - 1:
            send_ids()

    theirs_buf_send = mine_buf.at[1]
    mine_buf[1] = proj[1 - core].astype(BF16)
    swap = pair_copy(theirs_buf_send, theirs_buf, 2)
    swap.start()
    send_ids()
    mine = proj[core].astype(BF16)
    pl.when(forwards)(lambda: factor_copy().wait_recv())
    swap.wait_recv()
    theirs = theirs_buf[...]
    x_proj = jnp.where(core == 0, mine, theirs)
    d_proj = jnp.where(core == 0, theirs, mine)

    position = lax.broadcasted_iota(jnp.int32, (length, 1), 0)
    grads = []
    for s in range(seqs):
        rows = slice(s * length, (s + 1) * length)
        valid = (position < len_ref[s]).astype(BF16)
        grads.append(
            lax.dot_general(
                d_proj[rows], x_proj[rows] * valid, (((0,), (0,)), ((), ())), preferred_element_type=F32
            )
        )
    high, low = split(jnp.concatenate(grads, axis=1))
    left = jnp.dot(
        jnp.concatenate([halves[1, 0], halves[1, 0], halves[1, 1]], axis=1),
        jnp.concatenate([high, low, high], axis=0),
        preferred_element_type=F32,
    )
    high, low = split(jnp.concatenate([left[:, s * rank : (s + 1) * rank] for s in range(seqs)], axis=0))
    whites = jnp.dot(
        jnp.concatenate([high, low, high], axis=1),
        jnp.concatenate([halves[0, 0], halves[0, 0], halves[0, 1]], axis=0),
        preferred_element_type=F32,
    ).reshape(seqs, n, per, rank)
    if per % 8 == 0 and block == seqs * per:
        wsend[...] = jnp.concatenate([whites[s] for s in range(seqs)], axis=1).astype(BF16)
    else:
        for s in range(seqs):
            wide_white[:, s * per : (s + 1) * per] = whites[s]
        wsend[...] = wide_white[...].astype(BF16)

    def exchange(src, dst, send_sem, recv_sem, j):
        copy = pltpu.make_async_remote_copy(
            src_ref=src, dst_ref=dst,
            send_sem=send_sem.at[j], recv_sem=recv_sem.at[j],
            device_id=peer(j), device_id_type=MESH,
        )
        copy.start()
        return copy

    white_copies = [
        exchange(wsend.at[xor(me, j)], wrecv.at[me], ws_sem, wr_sem, j) for j in range(n - 1, 0, -1)
    ]
    wrecv[me] = wsend[me]
    bank_load.wait()
    for copy in white_copies:
        copy.wait_recv()
    white[...] = wrecv[...].astype(F32).reshape(n * block, rank)

    columns = jnp.concatenate(
        [
            jnp.concatenate(
                [white[pl.ds(s * per + a, n, stride=block), :] for s in range(seqs)], axis=0
            ).astype(BF16)
            for a in range(per)
        ],
        axis=1,
    )

    def partial(target):
        rows = bank[pl.ds(pl.multiple_of(target * queries, queries), psend.shape[2])]
        return lax.dot_general(columns, rows, (((1,), (1,)), ((), ())), preferred_element_type=F32)

    score_copies = []
    for j in range(n - 1, 0, -1):
        psend[j] = partial(xor(me, j)).astype(BF16)
        score_copies.append(exchange(psend.at[j], precv.at[j], ps_sem, pr_sem, j))
    total = partial(me)
    for j in range(1, n):
        id_copy(xor(me, j), me).wait_recv()
    ids = jnp.concatenate([idbuf[:, s, :] for s in range(seqs)], axis=0)[:, :1]
    held = n * seqs
    one_hot = (ids == lax.broadcasted_iota(jnp.int32, (held, held), 1)).astype(BF16)
    for make in all_sends:
        make().wait_send()

    def drain(makes):
        for make in makes:
            make().wait_send()

    for which, makes in forward_sends:
        pl.when(which)(functools.partial(drain, makes))
    pl.when(jnp.logical_not(forwards))(lambda: factor_copy().wait_send())
    for copy in [x_pair[0], swap] + white_copies:
        copy.wait_send()
    for j in range(1, n):
        id_copy(me, xor(me, j)).wait_send()
    for copy in score_copies:
        copy.wait_recv()
    for j in range(n - 1, 0, -1):
        total += precv[j].astype(F32)
    placed = lax.dot_general(
        one_hot, total.astype(BF16), (((0,), (0,)), ((), ())), preferred_element_type=F32
    )
    out_ref[...] = placed[:, :queries].astype(BF16)
    for copy in score_copies:
        copy.wait_send()


def solution(mesh):
    n = mesh.shape["coord"]
    assert mesh.shape["groups"] == 2
    chips = n // 2
    slow = 1
    while slow * slow < chips:
        slow *= 2
    fast = chips // slow

    def body(activations, out_grads, proj_in, proj_out, cov_in, cov_out, lengths, seq_ids, bank):
        seqs, length, width = activations.shape
        shard, rank = proj_in.shape
        per = bank.shape[1] // rank
        queries = bank.shape[0] // n
        wide = -(-queries // 128) * 128
        block = -(-(seqs * per) // 16) * 16
        held = n * seqs
        sends = 2 * (1 + fast) + 4 * slow + 2 * (slow - 1) * 2 * fast + 2 * slow * fast
        vmem = pl.BlockSpec(memory_space=pltpu.VMEM)
        hbm = pl.BlockSpec(memory_space=pltpu.HBM)
        dma = pltpu.SemaphoreType.DMA
        return pl.pallas_call(
            functools.partial(kernel, n, slow, fast),
            out_shape=jax.ShapeDtypeStruct((held, queries), BF16),
            in_specs=[hbm] * 9,
            out_specs=vmem,
            scratch_shapes=[
                pltpu.SMEM((seqs,), jnp.int32),
                pltpu.SMEM((seqs,), jnp.int32),
                pltpu.VMEM((2, seqs * length, width), BF16),
                pltpu.VMEM((2, seqs * length, rank), F32),
                pltpu.VMEM((n, shard, rank), BF16),
                pltpu.VMEM((shard, rank), BF16),
                pltpu.VMEM((bank.shape[0] + wide - queries, bank.shape[1]), BF16),
                pltpu.VMEM((2, rank, rank), F32),
                pltpu.VMEM((2, 2, rank, rank), BF16),
                pltpu.VMEM((2, seqs * length, rank), BF16),
                pltpu.VMEM((seqs * length, rank), BF16),
                pltpu.VMEM((n, seqs, 128), jnp.int32),
                pltpu.VMEM((n, block, rank), F32),
                pltpu.VMEM((n, block, rank), BF16),
                pltpu.VMEM((n, block, rank), BF16),
                pltpu.VMEM((n * block, rank), F32),
                pltpu.VMEM((n, held, wide), BF16),
                pltpu.VMEM((n, held, wide), BF16),
                dma((8,)),
                dma((sends * PARTS,)), dma((n, PARTS)), pltpu.SemaphoreType.REGULAR((max(slow, 2), 2)),
                dma((3,)), dma((3,)), dma((n,)), dma((n,)),
                dma((n,)), dma((n,)), dma((n,)), dma((n,)),
            ],
            compiler_params=pltpu.CompilerParams(
                collective_id=0, has_side_effects=True, vmem_limit_bytes=48 * 2**20
            ),
        )(*(
            pltpu.with_memory_space_constraint(array, pltpu.HBM)
            for array in (
                activations.reshape(seqs * length, width), out_grads.reshape(seqs * length, width),
                proj_in, proj_out, cov_in, cov_out, lengths, seq_ids, bank,
            )
        ))

    in_specs = (
        P(("groups", "coord"), None, None),
        P(("groups", "coord"), None, None),
        P("coord", None),
        P("coord", None),
        P(),
        P(),
        P(("groups", "coord")),
        P(("groups", "coord")),
        P(None, "coord"),
    )
    return jax.shard_map(body, mesh=mesh, in_specs=in_specs, out_specs=P("groups", "coord"), check_vma=False)
```

```python
import functools

import jax
import jax.numpy as jnp
from jax import lax
from jax.experimental import pallas as pl
from jax.experimental.pallas import tpu as pltpu
from jax.sharding import PartitionSpec as P

MESH = pl.DeviceIdType.MESH
F32 = jnp.float32
BF16 = jnp.bfloat16
PANEL = 8
PARTS = 1
EARLY = 3


def xor(value, mask):
    bit = 1
    result = value
    while bit <= mask:
        if mask & bit:
            result = result + bit - 2 * bit * ((value // bit) % 2)
        bit *= 2
    return result


def start_factor(cov):
    size = cov.shape[0]
    rows = lax.broadcasted_iota(jnp.int32, (size, size), 0)
    lanes = lax.broadcasted_iota(jnp.int32, (size, size), 1)
    diagonal = jnp.where(rows == lanes, cov, 0.0)
    damping = 0.1 * jnp.sum(diagonal) / size
    return jnp.where(rows == lanes, cov + damping, cov)


def eliminate_panel(matrix):
    size = matrix.shape[0]
    top, rest = matrix[:PANEL], matrix[PANEL:]
    lane = lax.broadcasted_iota(jnp.int32, (PANEL, size), 1)
    sub = lax.broadcasted_iota(jnp.int32, (PANEL, size), 0)
    pivots = [jnp.broadcast_to(top[:, r : r + 1], (PANEL, size)) for r in range(PANEL)]
    top = jnp.where(lane < PANEL, jnp.where(lane == sub, 1.0, 0.0), top)
    for r in range(PANEL):
        factor = pivots[r]
        inverse = 1.0 / factor[r : r + 1]

        def reduced(value):
            scaled = value[r : r + 1] * inverse
            return jnp.where(sub == r, scaled, value - factor * scaled)

        top = reduced(top)
        for later in range(r + 1, PANEL):
            pivots[later] = reduced(pivots[later])
    column = rest
    rest = jnp.where(lane[:1] < PANEL, 0.0, rest)
    for r in range(PANEL):
        rest = rest - column[:, r : r + 1] * top[r : r + 1]
    whole = jnp.concatenate([rest, top], axis=0)
    return pltpu.roll(whole, size - PANEL, 1)


def split(value):
    high = value.astype(BF16)
    return high, (value - high.astype(F32)).astype(BF16)


def kernel(
    n, slow, fast,
    act_ref, og_ref, pin_ref, pout_ref, cin_ref, cout_ref, len_hbm, ids_hbm, bank_ref,
    out_ref, len_ref, ids_ref,
    x, proj, w, stage, bank, factor, halves, mine_buf, theirs_buf, idbuf, wide_white, wsend, wrecv, white, psend, precv,
    load_sem, gs_sem, gr_sem, relay_sem, pair_send, pair_recv, is_sem, ir_sem, ws_sem, wr_sem, ps_sem, pr_sem,
):
    group = lax.axis_index("groups")
    me = lax.axis_index("coord")
    core = me % 2
    seqs = len_ref.shape[0]
    length = x.shape[1] // seqs
    rank = cin_ref.shape[0]
    shard = pin_ref.shape[0]
    queries = out_ref.shape[1]
    per = bank_ref.shape[1] // rank
    block = wsend.shape[1]
    level = me // (2 * fast)
    forwards = core == group
    solves = core != group
    home = me // 2

    def both(first, second):
        pl.when(core == 0)(first)
        pl.when(core == 1)(second)

    def load(src, dst, at):
        return pltpu.make_async_copy(src, dst, load_sem.at[at])

    own_w = [load(pin_ref, w.at[me], 0), load(pout_ref, w.at[me], 0)]
    own_s = [load(pout_ref, stage, 1), load(pin_ref, stage, 1)]
    own_f = [load(cin_ref, factor.at[0], 2), load(cout_ref, factor.at[1], 7)]
    own_x = [load(act_ref, x.at[core], 3), load(og_ref, x.at[core], 3)]
    for pair in (own_w, own_s):
        both(pair[0].start, pair[1].start)
    own_f[0].start()
    own_f[1].start()
    len_load, ids_load = load(len_hbm, len_ref, 4), load(ids_hbm, ids_ref, 5)
    bank_load = load(bank_ref, bank.at[pl.ds(0, bank_ref.shape[0])], 6)
    len_load.start()
    ids_load.start()

    fasts = [2 * b for b in range(1, fast)]
    ranks = range(1, slow)
    early = ranks[:EARLY]
    twin = (1 - group, me)
    chip = 2 * fast
    near = [xor(me, chip * a) for a in range(slow)]
    inner = jnp.minimum(level, 1) * jnp.minimum(slow - 1 - level, 1)
    if slow == 4:
        near[2:] = [near[2] + inner * (near[3] - near[2]), near[3] + inner * (near[2] - near[3])]

    def slot(rank_at, off):
        return xor(near[rank_at], off)

    def peer(mask):
        return (group, xor(me, mask))

    barrier = pltpu.get_barrier_semaphore()

    def signal(semaphore, to):
        pl.semaphore_signal(semaphore, inc=1, device_id=to, device_id_type=MESH)

    below, above = (group, me - 2 * fast), (group, me + 2 * fast)
    has_below, has_above = level > 0, level < slow - 1
    pl.when(has_below)(lambda: signal(barrier, below))
    pl.when(has_above)(lambda: signal(barrier, above))
    signal(barrier, twin)
    for mask in fasts + [1]:
        signal(barrier, peer(mask))
    both(own_x[0].start, own_x[1].start)
    bank_load.start()

    own_w[0].wait()
    own_s[0].wait()
    pl.semaphore_wait(barrier, 1 + fast + jnp.minimum(level, 1) + jnp.minimum(slow - 1 - level, 1))

    piece = shard // PARTS
    count = [0]
    all_sends, forward_sends = [], []

    def shard_copy(place, part, to, at, src=None):
        rows = pl.ds(part * piece, piece)
        return pltpu.make_async_remote_copy(
            src_ref=w.at[place, rows] if src is None else src.at[rows], dst_ref=w.at[place, rows],
            send_sem=gs_sem.at[at], recv_sem=gr_sem.at[place, part],
            device_id=to, device_id_type=MESH,
        )

    def send(source, part, to, sink, src=None):
        at = count[0]

        def make():
            device = (1 - group if to[0] else group, slot(to[1], to[2]))
            return shard_copy(slot(*source), part, device, at, src)

        count[0] += 1
        make().start()
        sink.append(make)

    def arrived(rank_at, off, parts=range(PARTS)):
        for part in parts:
            shard_copy(slot(rank_at, off), part, peer(1), 0).wait_recv()

    def pair_copy(src, dst, at):
        return pltpu.make_async_remote_copy(
            src_ref=src, dst_ref=dst, send_sem=pair_send.at[at], recv_sem=pair_recv.at[at],
            device_id=peer(1), device_id_type=MESH,
        )

    def along(rank_at, sources, which):
        group_of = []

        @pl.when(which)
        def _():
            for source in sources:
                for part in range(PARTS):
                    send((0, source), part, (0, rank_at, 0), group_of)

        forward_sends.append((which, group_of))

    def relay(step):
        @pl.when(forwards)
        def _():
            pl.when(has_below)(lambda: signal(relay_sem.at[step, 0], below))
            pl.when(has_above)(lambda: signal(relay_sem.at[step, 1], above))

    def relayed(step):
        @pl.when(forwards)
        def _():
            pl.when(has_above)(lambda: pl.semaphore_wait(relay_sem.at[step, 0], 1))
            pl.when(has_below)(lambda: pl.semaphore_wait(relay_sem.at[step, 1], 1))

    for part in range(PARTS):
        send((0, 0), part, (0, 0, 1), all_sends, stage)
    if slow > 2:
        relay(1)
    middle = jnp.logical_and(forwards, inner == 1)
    outer = jnp.logical_and(forwards, inner == 0)
    special = slow == 4
    if slow > 1:
        along(1, [0], forwards)
    if special:
        along(2, [0], middle)
    for part in range(PARTS):
        for mask in fasts:
            send((0, 0), part, (0, 0, mask), all_sends)
    x_pair = [pair_copy(og_ref, x.at[core], 0), pair_copy(act_ref, x.at[core], 0)]
    both(x_pair[0].start, x_pair[1].start)
    own_f[0].wait()
    own_f[1].wait()

    def step(_, carry):
        first, second = factor[0], factor[1]
        factor[0] = eliminate_panel(first)
        factor[1] = eliminate_panel(second)
        return carry

    arrived(0, 1)
    if slow > 1:
        along(1, [1], forwards)
    if special:
        along(2, [1], middle)
    for part in range(PARTS):
        for mask in fasts:
            send((0, 1), part, (0, 0, mask), all_sends)
    for at in range(1, slow - 1):
        relayed(at)
        if at + 1 < slow - 1:
            relay(at + 1)
        if not special:
            along(at + 1, [0, 1], forwards)
        elif at == 1:
            along(3, [0, 1], middle)
            along(2, [0, 1], outer)
        else:
            along(3, [0, 1], outer)

    len_load.wait()
    ids_load.wait()
    for s in range(seqs):
        idbuf[home, core, s : s + 1] = jnp.full((1, idbuf.shape[3]), ids_ref[s], jnp.int32)
    tail = bank.shape[0] - bank_ref.shape[0]
    if tail:
        bank[bank_ref.shape[0] :] = jnp.zeros((tail, bank.shape[1]), BF16)
    if block > 2 * seqs * per:
        wide_white[...] = jnp.zeros_like(wide_white)

    @pl.when(solves)
    def _():
        for at in range(2):
            factor[at] = start_factor(factor[at])
        lax.fori_loop(0, rank // PANEL, step, 0)
        for at in range(2):
            high, low = split(factor[at])
            halves[at, 0] = high
            halves[at, 1] = low

    known = []

    def id_copy(place, to):
        return pltpu.make_async_remote_copy(
            src_ref=idbuf.at[place // 2, place % 2], dst_ref=idbuf.at[place // 2, place % 2],
            send_sem=is_sem.at[to], recv_sem=ir_sem.at[place],
            device_id=(group, to), device_id_type=MESH,
        )

    def send_ids():
        for source in known:
            id_copy(me, slot(*source)).start()
        known.clear()

    def from_near():
        for b in fasts:
            for c in range(2):
                arrived(0, b + c)
                known.append((0, b + c))
        known.append((0, 1))

    def from_slow(rank_at):
        for c in range(2):
            for part in range(PARTS):
                arrived(rank_at, c, [part])
                group_of = []

                @pl.when(forwards)
                def _():
                    source = (rank_at, c)
                    for b in fasts:
                        send(source, part, (0, 0, b), group_of)
                    send(source, part, (1, 0, 0), group_of)
                    if rank_at not in early:
                        for b in fasts:
                            send(source, part, (1, 0, b), group_of)

                forward_sends.append((forwards, group_of))
            known.append((rank_at, c))

    def from_fast(rank_at):
        for b in fasts:
            for c in range(2):
                for part in range(PARTS):
                    arrived(rank_at, b + c, [part])
                    if rank_at in early:
                        group_of = []

                        @pl.when(forwards)
                        def _():
                            send((rank_at, b + c), part, (1, 0, 0), group_of)

                        forward_sends.append((forwards, group_of))
                known.append((rank_at, b + c))

    span = n // slow * shard

    def add(first, slots, shards, columns):
        value = jnp.dot(
            x[:, :, columns].reshape(2 * seqs * length, -1), w[shards].reshape(slots * shard, rank),
            preferred_element_type=F32,
        ).reshape(2, seqs * length, rank)
        if first:
            proj[...] = value
        else:
            proj[...] += value

    def load_x():
        own_x[0].wait()
        x_pair[0].wait_recv()

    def project(rank_at):
        at = near[rank_at] // chip
        add(rank_at == 0, chip, pl.ds(at * chip, chip), pl.ds(pl.multiple_of(at * span, 128), span))

    def project_pair(rank_at, off):
        at = slot(rank_at, off) // 2
        add(False, 2, pl.ds(at * 2, 2), pl.ds(pl.multiple_of(at * 2 * shard, 128), 2 * shard))

    pairs = (2 * shard) % 128 == 0 and slow > 1
    last = slow - 1

    def on_solver(event, *args):
        pl.when(solves)(functools.partial(event, *args))

    from_near()
    send_ids()
    for at in ranks:
        from_slow(at)
        if at == 1:
            load_x()
        else:
            from_fast(at - 1)
        send_ids()
        on_solver(project, at - 1)
    if slow > 1:
        if pairs:
            on_solver(project_pair, last, 0)
        from_fast(last)
    else:
        load_x()

    @pl.when(forwards)
    def _():
        for at in range(slow):
            project(at)

    @pl.when(solves)
    def _():
        if pairs:
            for b in fasts:
                project_pair(last, b)
        else:
            project(last)

    position = lax.broadcasted_iota(jnp.int32, (length, 1), 0)

    def masked():
        for s in range(seqs):
            rows = slice(s * length, (s + 1) * length)
            valid = (position < len_ref[s]).astype(F32)
            proj[core, rows] = proj[core, rows] * valid
        return proj[...].astype(BF16)

    def white_at(place, j, to):
        return pltpu.make_async_remote_copy(
            src_ref=wsend.at[to], dst_ref=wrecv.at[place],
            send_sem=ws_sem.at[j], recv_sem=wr_sem.at[place],
            device_id=(group, to), device_id_type=MESH,
        )

    def white_copy(j):
        return white_at(home, j, xor(me, j))

    def swap():
        return pair_copy(mine_buf, theirs_buf, 2)

    @pl.when(forwards)
    def _():
        mine_buf[...] = masked()
        swap().start()

    send_ids()

    @pl.when(solves)
    def _():
        mine = masked()
        swap().wait_recv()
        theirs = theirs_buf[...]
        x_proj = jnp.where(core == 0, mine, theirs)
        d_proj = jnp.where(core == 0, theirs, mine)
        grads = []
        for s in range(2 * seqs):
            rows = slice(s % seqs * length, (s % seqs + 1) * length)
            grads.append(
                lax.dot_general(
                    d_proj[s // seqs, rows], x_proj[s // seqs, rows], (((0,), (0,)), ((), ())),
                    preferred_element_type=F32,
                )
            )
        high, low = split(jnp.concatenate(grads, axis=1))
        left = jnp.dot(
            jnp.concatenate([halves[1, 0], halves[1, 0], halves[1, 1]], axis=1),
            jnp.concatenate([high, low, high], axis=0),
            preferred_element_type=F32,
        )
        high, low = split(jnp.concatenate([left[:, s * rank : (s + 1) * rank] for s in range(2 * seqs)], axis=0))
        whites = jnp.dot(
            jnp.concatenate([high, low, high], axis=1),
            jnp.concatenate([halves[0, 0], halves[0, 0], halves[0, 1]], axis=0),
            preferred_element_type=F32,
        ).reshape(2 * seqs, n, per, rank)
        if per % 8 == 0 and block == 2 * seqs * per:
            wsend[...] = jnp.concatenate([whites[s] for s in range(2 * seqs)], axis=1).astype(BF16)
        else:
            for s in range(2 * seqs):
                wide_white[:, s * per : (s + 1) * per] = whites[s]
            wsend[...] = wide_white[...].astype(BF16)
        for j in range(n - 1, 0, -1):
            white_copy(j).start()
        wrecv[home] = wsend[me]

    def exchange(src, dst, send_sem, recv_sem, j):
        copy = pltpu.make_async_remote_copy(
            src_ref=src, dst_ref=dst,
            send_sem=send_sem.at[j], recv_sem=recv_sem.at[j],
            device_id=peer(j), device_id_type=MESH,
        )
        copy.start()
        return copy

    bank_load.wait()

    def white_arrived(place):
        white_at(place, 0, me).wait_recv()

    pl.when(forwards)(lambda: white_arrived(home))
    for j in range(1, n // 2):
        white_arrived(xor(home, j))
    white[...] = wrecv[...].astype(F32).reshape(n // 2 * block, rank)

    columns = jnp.concatenate(
        [
            jnp.concatenate(
                [white[pl.ds(s * per + a, n // 2, stride=block), :] for s in range(2 * seqs)], axis=0
            ).astype(BF16)
            for a in range(per)
        ],
        axis=1,
    )

    def partial(target):
        rows = bank[pl.ds(pl.multiple_of(target * queries, queries), psend.shape[2])]
        return lax.dot_general(columns, rows, (((1,), (1,)), ((), ())), preferred_element_type=F32)

    score_copies = []
    for j in range(n - 1, 0, -1):
        psend[j] = partial(xor(me, j)).astype(BF16)
        score_copies.append(exchange(psend.at[j], precv.at[j], ps_sem, pr_sem, j))
    total = partial(me)
    for j in range(1, n):
        id_copy(xor(me, j), me).wait_recv()
    ids = jnp.concatenate([idbuf[:, s // seqs, s % seqs, :] for s in range(2 * seqs)], axis=0)[:, :1]
    held = n * seqs
    one_hot = (ids == lax.broadcasted_iota(jnp.int32, (held, held), 1)).astype(BF16)
    for make in all_sends:
        make().wait_send()

    def drain(makes):
        for make in makes:
            make().wait_send()

    for which, makes in forward_sends:
        pl.when(which)(functools.partial(drain, makes))
    x_pair[0].wait_send()
    pl.when(forwards)(lambda: swap().wait_send())

    @pl.when(solves)
    def _():
        for j in range(1, n):
            white_copy(j).wait_send()

    for j in range(1, n):
        id_copy(me, xor(me, j)).wait_send()
    for copy in score_copies:
        copy.wait_recv()
    for j in range(n - 1, 0, -1):
        total += precv[j].astype(F32)
    placed = lax.dot_general(
        one_hot, total.astype(BF16), (((0,), (0,)), ((), ())), preferred_element_type=F32
    )
    out_ref[...] = placed[:, :queries].astype(BF16)
    for copy in score_copies:
        copy.wait_send()


def solution(mesh):
    n = mesh.shape["coord"]
    assert mesh.shape["groups"] == 2
    chips = n // 2
    slow = 1
    while slow * slow < chips:
        slow *= 2
    fast = chips // slow

    def body(activations, out_grads, proj_in, proj_out, cov_in, cov_out, lengths, seq_ids, bank):
        seqs, length, width = activations.shape
        shard, rank = proj_in.shape
        per = bank.shape[1] // rank
        queries = bank.shape[0] // n
        wide = -(-queries // 128) * 128
        block = -(-(2 * seqs * per) // 16) * 16
        held = n * seqs
        sends = 2 * (1 + fast) + 4 * slow + 2 * (slow - 1) * 2 * fast + 2 * slow * fast
        vmem = pl.BlockSpec(memory_space=pltpu.VMEM)
        hbm = pl.BlockSpec(memory_space=pltpu.HBM)
        dma = pltpu.SemaphoreType.DMA
        return pl.pallas_call(
            functools.partial(kernel, n, slow, fast),
            out_shape=jax.ShapeDtypeStruct((held, queries), BF16),
            in_specs=[hbm] * 9,
            out_specs=vmem,
            scratch_shapes=[
                pltpu.SMEM((seqs,), jnp.int32),
                pltpu.SMEM((seqs,), jnp.int32),
                pltpu.VMEM((2, seqs * length, width), BF16),
                pltpu.VMEM((2, seqs * length, rank), F32),
                pltpu.VMEM((n, shard, rank), BF16),
                pltpu.VMEM((shard, rank), BF16),
                pltpu.VMEM((bank.shape[0] + wide - queries, bank.shape[1]), BF16),
                pltpu.VMEM((2, rank, rank), F32),
                pltpu.VMEM((2, 2, rank, rank), BF16),
                pltpu.VMEM((2, seqs * length, rank), BF16),
                pltpu.VMEM((2, seqs * length, rank), BF16),
                pltpu.VMEM((n // 2, 2, seqs, 128), jnp.int32),
                pltpu.VMEM((n, block, rank), F32),
                pltpu.VMEM((n, block, rank), BF16),
                pltpu.VMEM((n // 2, block, rank), BF16),
                pltpu.VMEM((n // 2 * block, rank), F32),
                pltpu.VMEM((n, held, wide), BF16),
                pltpu.VMEM((n, held, wide), BF16),
                dma((8,)),
                dma((sends * PARTS,)), dma((n, PARTS)), pltpu.SemaphoreType.REGULAR((max(slow, 2), 2)),
                dma((3,)), dma((3,)), dma((n,)), dma((n,)),
                dma((n,)), dma((n,)), dma((n,)), dma((n,)),
            ],
            compiler_params=pltpu.CompilerParams(
                collective_id=0, has_side_effects=True, vmem_limit_bytes=48 * 2**20
            ),
        )(*(
            pltpu.with_memory_space_constraint(array, pltpu.HBM)
            for array in (
                activations.reshape(seqs * length, width), out_grads.reshape(seqs * length, width),
                proj_in, proj_out, cov_in, cov_out, lengths, seq_ids, bank,
            )
        ))

    in_specs = (
        P(("groups", "coord"), None, None),
        P(("groups", "coord"), None, None),
        P("coord", None),
        P("coord", None),
        P(),
        P(),
        P(("groups", "coord")),
        P(("groups", "coord")),
        P(None, "coord"),
    )
    return jax.shard_map(body, mesh=mesh, in_specs=in_specs, out_specs=P("groups", "coord"), check_vma=False)
```

```python
import functools

import jax
import jax.numpy as jnp
from jax import lax
from jax.experimental import pallas as pl
from jax.experimental.pallas import tpu as pltpu
from jax.sharding import PartitionSpec as P

MESH = pl.DeviceIdType.MESH
F32 = jnp.float32
BF16 = jnp.bfloat16
PANEL = 8
PARTS = 1
EARLY = 3


def xor(value, mask):
    bit = 1
    result = value
    while bit <= mask:
        if mask & bit:
            result = result + bit - 2 * bit * ((value // bit) % 2)
        bit *= 2
    return result


def start_factor(cov):
    size = cov.shape[0]
    rows = lax.broadcasted_iota(jnp.int32, (size, size), 0)
    lanes = lax.broadcasted_iota(jnp.int32, (size, size), 1)
    diagonal = jnp.where(rows == lanes, cov, 0.0)
    damping = 0.1 * jnp.sum(diagonal) / size
    return jnp.where(rows == lanes, cov + damping, cov)


def eliminate_panel(matrix):
    size = matrix.shape[0]
    top, rest = matrix[:PANEL], matrix[PANEL:]
    lane = lax.broadcasted_iota(jnp.int32, (PANEL, size), 1)
    sub = lax.broadcasted_iota(jnp.int32, (PANEL, size), 0)
    pivots = [jnp.broadcast_to(top[:, r : r + 1], (PANEL, size)) for r in range(PANEL)]
    top = jnp.where(lane < PANEL, jnp.where(lane == sub, 1.0, 0.0), top)
    for r in range(PANEL):
        factor = pivots[r]
        inverse = 1.0 / factor[r : r + 1]

        def reduced(value):
            scaled = value[r : r + 1] * inverse
            return jnp.where(sub == r, scaled, value - factor * scaled)

        top = reduced(top)
        for later in range(r + 1, PANEL):
            pivots[later] = reduced(pivots[later])
    column = rest
    rest = jnp.where(lane[:1] < PANEL, 0.0, rest)
    for r in range(PANEL):
        rest = rest - column[:, r : r + 1] * top[r : r + 1]
    whole = jnp.concatenate([rest, top], axis=0)
    return pltpu.roll(whole, size - PANEL, 1)


def split(value):
    high = value.astype(BF16)
    return high, (value - high.astype(F32)).astype(BF16)


def kernel(
    n, slow, fast,
    act_ref, og_ref, pin_ref, pout_ref, cin_ref, cout_ref, len_hbm, ids_hbm, bank_ref,
    out_ref, len_ref, ids_ref,
    x, proj, w, stage, bank, factor, halves, mine_buf, theirs_buf, idbuf, wide_white, wsend, wrecv, white, psend, precv,
    load_sem, gs_sem, gr_sem, relay_sem, pair_send, pair_recv, is_sem, ir_sem, ws_sem, wr_sem, ps_sem, pr_sem,
):
    group = lax.axis_index("groups")
    me = lax.axis_index("coord")
    core = me % 2
    seqs = len_ref.shape[0]
    length = x.shape[1] // seqs
    rank = cin_ref.shape[0]
    shard = pin_ref.shape[0]
    queries = out_ref.shape[1]
    per = bank_ref.shape[1] // rank
    block = wsend.shape[1]
    level = me // (2 * fast)
    forwards = core == group
    solves = core != group
    home = me // 2

    def both(first, second):
        pl.when(core == 0)(first)
        pl.when(core == 1)(second)

    def load(src, dst, at):
        return pltpu.make_async_copy(src, dst, load_sem.at[at])

    own_w = [load(pin_ref, w.at[me], 0), load(pout_ref, w.at[me], 0)]
    own_s = [load(pout_ref, stage, 1), load(pin_ref, stage, 1)]
    own_f = [load(cin_ref, factor.at[0], 2), load(cout_ref, factor.at[1], 7)]
    own_x = [load(act_ref, x.at[core], 3), load(og_ref, x.at[core], 3)]
    for pair in (own_w, own_s):
        both(pair[0].start, pair[1].start)
    own_f[0].start()
    own_f[1].start()
    len_load, ids_load = load(len_hbm, len_ref, 4), load(ids_hbm, ids_ref, 5)
    bank_load = load(bank_ref, bank, 6)
    len_load.start()
    ids_load.start()

    fasts = [2 * b for b in range(1, fast)]
    ranks = range(1, slow)
    early = ranks[:EARLY]
    twin = (1 - group, me)
    chip = 2 * fast
    near = [xor(me, chip * a) for a in range(slow)]
    inner = jnp.minimum(level, 1) * jnp.minimum(slow - 1 - level, 1)
    if slow == 4:
        near[2:] = [near[2] + inner * (near[3] - near[2]), near[3] + inner * (near[2] - near[3])]

    def slot(rank_at, off):
        return xor(near[rank_at], off)

    def peer(mask):
        return (group, xor(me, mask))

    barrier = pltpu.get_barrier_semaphore()

    def signal(semaphore, to):
        pl.semaphore_signal(semaphore, inc=1, device_id=to, device_id_type=MESH)

    below, above = (group, me - 2 * fast), (group, me + 2 * fast)
    has_below, has_above = level > 0, level < slow - 1
    pl.when(has_below)(lambda: signal(barrier, below))
    pl.when(has_above)(lambda: signal(barrier, above))
    signal(barrier, twin)
    for mask in fasts + [1]:
        signal(barrier, peer(mask))
    both(own_x[0].start, own_x[1].start)
    bank_load.start()

    own_w[0].wait()
    own_s[0].wait()
    pl.semaphore_wait(barrier, 1 + fast + jnp.minimum(level, 1) + jnp.minimum(slow - 1 - level, 1))

    piece = shard // PARTS
    count = [0]
    all_sends, forward_sends = [], []

    def shard_copy(place, part, to, at, src=None):
        rows = pl.ds(part * piece, piece)
        return pltpu.make_async_remote_copy(
            src_ref=w.at[place, rows] if src is None else src.at[rows], dst_ref=w.at[place, rows],
            send_sem=gs_sem.at[at], recv_sem=gr_sem.at[place, part],
            device_id=to, device_id_type=MESH,
        )

    def send(source, part, to, sink, src=None):
        at = count[0]

        def make():
            device = (1 - group if to[0] else group, slot(to[1], to[2]))
            return shard_copy(slot(*source), part, device, at, src)

        count[0] += 1
        make().start()
        sink.append(make)

    def arrived(rank_at, off, parts=range(PARTS)):
        for part in parts:
            shard_copy(slot(rank_at, off), part, peer(1), 0).wait_recv()

    def pair_copy(src, dst, at):
        return pltpu.make_async_remote_copy(
            src_ref=src, dst_ref=dst, send_sem=pair_send.at[at], recv_sem=pair_recv.at[at],
            device_id=peer(1), device_id_type=MESH,
        )

    def along(rank_at, sources, which):
        group_of = []

        @pl.when(which)
        def _():
            for source in sources:
                for part in range(PARTS):
                    send((0, source), part, (0, rank_at, 0), group_of)

        forward_sends.append((which, group_of))

    def relay(step):
        @pl.when(forwards)
        def _():
            pl.when(has_below)(lambda: signal(relay_sem.at[step, 0], below))
            pl.when(has_above)(lambda: signal(relay_sem.at[step, 1], above))

    def relayed(step):
        @pl.when(forwards)
        def _():
            pl.when(has_above)(lambda: pl.semaphore_wait(relay_sem.at[step, 0], 1))
            pl.when(has_below)(lambda: pl.semaphore_wait(relay_sem.at[step, 1], 1))

    for part in range(PARTS):
        send((0, 0), part, (0, 0, 1), all_sends, stage)
    if slow > 2:
        relay(1)
    middle = jnp.logical_and(forwards, inner == 1)
    outer = jnp.logical_and(forwards, inner == 0)
    special = slow == 4
    if slow > 1:
        along(1, [0], forwards)
    if special:
        along(2, [0], middle)
    for part in range(PARTS):
        for mask in fasts:
            send((0, 0), part, (0, 0, mask), all_sends)
    x_pair = [pair_copy(og_ref, x.at[core], 0), pair_copy(act_ref, x.at[core], 0)]
    both(x_pair[0].start, x_pair[1].start)
    own_f[0].wait()
    own_f[1].wait()

    def step(_, carry):
        first, second = factor[0], factor[1]
        factor[0] = eliminate_panel(first)
        factor[1] = eliminate_panel(second)
        return carry

    if slow > 2:
        relayed(1)
        if slow > 3:
            relay(2)
    if special:
        along(3, [0], middle)
        along(2, [0], outer)
    arrived(0, 1)
    if slow > 1:
        along(1, [1], forwards)
    if special:
        along(2, [1], middle)
    for part in range(PARTS):
        for mask in fasts:
            send((0, 1), part, (0, 0, mask), all_sends)
    for at in range(1, slow - 1):
        if at > 1:
            relayed(at)
            if at + 1 < slow - 1:
                relay(at + 1)
        if not special:
            along(at + 1, [0, 1], forwards)
        elif at == 1:
            along(3, [1], middle)
            along(2, [1], outer)
        else:
            along(3, [0, 1], outer)

    len_load.wait()
    ids_load.wait()
    for s in range(seqs):
        idbuf[home, core, s : s + 1] = jnp.full((1, idbuf.shape[3]), ids_ref[s], jnp.int32)
    if psend.shape[2] > queries:
        psend[...] = jnp.zeros_like(psend)
    if block > 2 * seqs * per:
        wide_white[...] = jnp.zeros_like(wide_white)

    @pl.when(solves)
    def _():
        for at in range(2):
            factor[at] = start_factor(factor[at])
        lax.fori_loop(0, rank // PANEL, step, 0)
        for at in range(2):
            high, low = split(factor[at])
            halves[at, 0] = high
            halves[at, 1] = low

    known = []

    def id_copy(place, to):
        return pltpu.make_async_remote_copy(
            src_ref=idbuf.at[place // 2, place % 2], dst_ref=idbuf.at[place // 2, place % 2],
            send_sem=is_sem.at[to], recv_sem=ir_sem.at[place],
            device_id=(group, to), device_id_type=MESH,
        )

    def send_ids():
        for source in known:
            id_copy(me, slot(*source)).start()
        known.clear()

    def from_near():
        for b in fasts:
            for c in range(2):
                arrived(0, b + c)
                known.append((0, b + c))
        known.append((0, 1))

    def from_slow(rank_at):
        for c in range(2):
            for part in range(PARTS):
                arrived(rank_at, c, [part])
                group_of = []

                @pl.when(forwards)
                def _():
                    source = (rank_at, c)
                    for b in fasts:
                        send(source, part, (0, 0, b), group_of)
                    send(source, part, (1, 0, 0), group_of)
                    if rank_at not in early:
                        for b in fasts:
                            send(source, part, (1, 0, b), group_of)

                forward_sends.append((forwards, group_of))
            known.append((rank_at, c))

    def from_fast(rank_at):
        for b in fasts:
            for c in range(2):
                for part in range(PARTS):
                    arrived(rank_at, b + c, [part])
                    if rank_at in early:
                        group_of = []

                        @pl.when(forwards)
                        def _():
                            send((rank_at, b + c), part, (1, 0, 0), group_of)

                        forward_sends.append((forwards, group_of))
                known.append((rank_at, b + c))

    span = n // slow * shard

    def add(first, slots, shards, columns):
        value = jnp.dot(
            x[:, :, columns].reshape(2 * seqs * length, -1), w[shards].reshape(slots * shard, rank),
            preferred_element_type=F32,
        ).reshape(2, seqs * length, rank)
        if first:
            proj[...] = value
        else:
            proj[...] += value

    def load_x():
        own_x[0].wait()
        x_pair[0].wait_recv()

    def project(rank_at):
        at = near[rank_at] // chip
        add(rank_at == 0, chip, pl.ds(at * chip, chip), pl.ds(pl.multiple_of(at * span, 128), span))

    def project_pair(rank_at, off):
        at = slot(rank_at, off) // 2
        add(False, 2, pl.ds(at * 2, 2), pl.ds(pl.multiple_of(at * 2 * shard, 128), 2 * shard))

    pairs = (2 * shard) % 128 == 0 and slow > 1
    last = slow - 1

    def on_solver(event, *args):
        pl.when(solves)(functools.partial(event, *args))

    if slow == 1 or len(early) < slow - 1:
        from_near()
        send_ids()
    for at in ranks:
        from_slow(at)
        if at == 1 and len(early) == slow - 1:
            from_near()
        if at == 1:
            load_x()
        else:
            from_fast(at - 1)
        send_ids()
        if at < slow - 1:
            project(at - 1)
        else:
            on_solver(project, at - 1)
    if slow > 1:
        if pairs:
            on_solver(project_pair, last, 0)
        from_fast(last)
    else:
        load_x()

    @pl.when(forwards)
    def _():
        for at in range(max(0, slow - 2), slow):
            project(at)

    @pl.when(solves)
    def _():
        if pairs:
            for b in fasts:
                project_pair(last, b)
        else:
            project(last)

    position = lax.broadcasted_iota(jnp.int32, (length, 1), 0)

    def masked():
        for s in range(seqs):
            rows = slice(s * length, (s + 1) * length)
            valid = (position < len_ref[s]).astype(F32)
            proj[core, rows] = proj[core, rows] * valid
        return proj[...].astype(BF16)

    def white_at(place, j, to):
        return pltpu.make_async_remote_copy(
            src_ref=wsend.at[to], dst_ref=wrecv.at[place],
            send_sem=ws_sem.at[j], recv_sem=wr_sem.at[place],
            device_id=(group, to), device_id_type=MESH,
        )

    def white_copy(j):
        return white_at(home, j, xor(me, j))

    def swap():
        return pair_copy(mine_buf, theirs_buf, 2)

    @pl.when(forwards)
    def _():
        mine_buf[...] = masked()
        swap().start()

    send_ids()

    @pl.when(solves)
    def _():
        mine = masked()
        swap().wait_recv()
        theirs = theirs_buf[...]
        x_proj = jnp.where(core == 0, mine, theirs)
        d_proj = jnp.where(core == 0, theirs, mine)
        grads = []
        for s in range(2 * seqs):
            rows = slice(s % seqs * length, (s % seqs + 1) * length)
            grads.append(
                lax.dot_general(
                    d_proj[s // seqs, rows], x_proj[s // seqs, rows], (((0,), (0,)), ((), ())),
                    preferred_element_type=F32,
                )
            )
        high, low = split(jnp.concatenate(grads, axis=1))
        left = jnp.dot(
            jnp.concatenate([halves[1, 0], halves[1, 0], halves[1, 1]], axis=1),
            jnp.concatenate([high, low, high], axis=0),
            preferred_element_type=F32,
        )
        high, low = split(jnp.concatenate([left[:, s * rank : (s + 1) * rank] for s in range(2 * seqs)], axis=0))
        whites = jnp.dot(
            jnp.concatenate([high, low, high], axis=1),
            jnp.concatenate([halves[0, 0], halves[0, 0], halves[0, 1]], axis=0),
            preferred_element_type=F32,
        ).reshape(2 * seqs, n, per, rank)
        if per % 8 == 0 and block == 2 * seqs * per:
            wsend[...] = jnp.concatenate([whites[s] for s in range(2 * seqs)], axis=1).astype(BF16)
        else:
            for s in range(2 * seqs):
                wide_white[:, s * per : (s + 1) * per] = whites[s]
            wsend[...] = wide_white[...].astype(BF16)
        for j in range(n - 1, 0, -1):
            white_copy(j).start()
        wrecv[home] = wsend[me]

    def exchange(src, dst, send_sem, recv_sem, j):
        copy = pltpu.make_async_remote_copy(
            src_ref=src, dst_ref=dst,
            send_sem=send_sem.at[j], recv_sem=recv_sem.at[j],
            device_id=peer(j), device_id_type=MESH,
        )
        copy.start()
        return copy

    bank_load.wait()

    def white_arrived(place):
        white_at(place, 0, me).wait_recv()

    pl.when(forwards)(lambda: white_arrived(home))
    for j in range(1, n // 2):
        white_arrived(xor(home, j))
    white[...] = wrecv[...].astype(F32).reshape(n // 2 * block, rank)

    columns = jnp.concatenate(
        [
            jnp.concatenate(
                [white[pl.ds(s * per + a, n // 2, stride=block), :] for s in range(2 * seqs)], axis=0
            ).astype(BF16)
            for a in range(per)
        ],
        axis=1,
    )

    def partial(target):
        rows = bank[pl.ds(pl.multiple_of(target * queries, queries), queries)]
        return lax.dot_general(columns, rows, (((1,), (1,)), ((), ())), preferred_element_type=F32)

    score_copies = []
    for j in range(n - 1, 0, -1):
        psend[j, :, :queries] = partial(xor(me, j)).astype(BF16)
        score_copies.append(exchange(psend.at[j], precv.at[j], ps_sem, pr_sem, j))
    total = partial(me)
    for j in range(1, n):
        id_copy(xor(me, j), me).wait_recv()
    ids = jnp.concatenate([idbuf[:, s // seqs, s % seqs, :] for s in range(2 * seqs)], axis=0)[:, :1]
    held = n * seqs
    one_hot = (ids == lax.broadcasted_iota(jnp.int32, (held, held), 1)).astype(BF16)
    for make in all_sends:
        make().wait_send()

    def drain(makes):
        for make in makes:
            make().wait_send()

    for which, makes in forward_sends:
        pl.when(which)(functools.partial(drain, makes))
    x_pair[0].wait_send()
    pl.when(forwards)(lambda: swap().wait_send())

    @pl.when(solves)
    def _():
        for j in range(1, n):
            white_copy(j).wait_send()

    for j in range(1, n):
        id_copy(me, xor(me, j)).wait_send()
    for j, copy in zip(range(n - 1, 0, -1), score_copies):
        copy.wait_recv()
        total += precv[j, :, :queries].astype(F32)
    placed = lax.dot_general(
        one_hot, total.astype(BF16), (((0,), (0,)), ((), ())), preferred_element_type=F32
    )
    out_ref[...] = placed.astype(BF16)
    for copy in score_copies:
        copy.wait_send()


def solution(mesh):
    n = mesh.shape["coord"]
    assert mesh.shape["groups"] == 2
    chips = n // 2
    slow = 1
    while slow * slow < chips:
        slow *= 2
    fast = chips // slow

    def body(activations, out_grads, proj_in, proj_out, cov_in, cov_out, lengths, seq_ids, bank):
        seqs, length, width = activations.shape
        shard, rank = proj_in.shape
        per = bank.shape[1] // rank
        queries = bank.shape[0] // n
        wide = -(-queries // 128) * 128
        block = -(-(2 * seqs * per) // 16) * 16
        held = n * seqs
        sends = 2 * (1 + fast) + 4 * slow + 2 * (slow - 1) * 2 * fast + 2 * slow * fast
        vmem = pl.BlockSpec(memory_space=pltpu.VMEM)
        hbm = pl.BlockSpec(memory_space=pltpu.HBM)
        dma = pltpu.SemaphoreType.DMA
        return pl.pallas_call(
            functools.partial(kernel, n, slow, fast),
            out_shape=jax.ShapeDtypeStruct((held, queries), BF16),
            in_specs=[hbm] * 9,
            out_specs=vmem,
            scratch_shapes=[
                pltpu.SMEM((seqs,), jnp.int32),
                pltpu.SMEM((seqs,), jnp.int32),
                pltpu.VMEM((2, seqs * length, width), BF16),
                pltpu.VMEM((2, seqs * length, rank), F32),
                pltpu.VMEM((n, shard, rank), BF16),
                pltpu.VMEM((shard, rank), BF16),
                pltpu.VMEM(bank.shape, BF16),
                pltpu.VMEM((2, rank, rank), F32),
                pltpu.VMEM((2, 2, rank, rank), BF16),
                pltpu.VMEM((2, seqs * length, rank), BF16),
                pltpu.VMEM((2, seqs * length, rank), BF16),
                pltpu.VMEM((n // 2, 2, seqs, 128), jnp.int32),
                pltpu.VMEM((n, block, rank), F32),
                pltpu.VMEM((n, block, rank), BF16),
                pltpu.VMEM((n // 2, block, rank), BF16),
                pltpu.VMEM((n // 2 * block, rank), F32),
                pltpu.VMEM((n, held, wide), BF16),
                pltpu.VMEM((n, held, wide), BF16),
                dma((8,)),
                dma((sends * PARTS,)), dma((n, PARTS)), pltpu.SemaphoreType.REGULAR((max(slow, 2), 2)),
                dma((3,)), dma((3,)), dma((n,)), dma((n,)),
                dma((n,)), dma((n,)), dma((n,)), dma((n,)),
            ],
            compiler_params=pltpu.CompilerParams(
                collective_id=0, has_side_effects=True, vmem_limit_bytes=48 * 2**20
            ),
        )(*(
            pltpu.with_memory_space_constraint(array, pltpu.HBM)
            for array in (
                activations.reshape(seqs * length, width), out_grads.reshape(seqs * length, width),
                proj_in, proj_out, cov_in, cov_out, lengths, seq_ids, bank,
            )
        ))

    in_specs = (
        P(("groups", "coord"), None, None),
        P(("groups", "coord"), None, None),
        P("coord", None),
        P("coord", None),
        P(),
        P(),
        P(("groups", "coord")),
        P(("groups", "coord")),
        P(None, "coord"),
    )
    return jax.shard_map(body, mesh=mesh, in_specs=in_specs, out_specs=P("groups", "coord"), check_vma=False)
```

```python
import functools

import jax
import jax.numpy as jnp
from jax import lax
from jax.experimental import pallas as pl
from jax.experimental.pallas import tpu as pltpu
from jax.sharding import PartitionSpec as P

MESH = pl.DeviceIdType.MESH
F32 = jnp.float32
BF16 = jnp.bfloat16
PANEL = 8
PARTS = 1
EARLY = 3


def xor(value, mask):
    bit = 1
    result = value
    while bit <= mask:
        if mask & bit:
            result = result + bit - 2 * bit * ((value // bit) % 2)
        bit *= 2
    return result


def start_factor(cov):
    size = cov.shape[0]
    rows = lax.broadcasted_iota(jnp.int32, (size, size), 0)
    lanes = lax.broadcasted_iota(jnp.int32, (size, size), 1)
    diagonal = jnp.where(rows == lanes, cov, 0.0)
    damping = 0.1 * jnp.sum(diagonal) / size
    return jnp.where(rows == lanes, cov + damping, cov)


def eliminate_panel(matrix):
    size = matrix.shape[0]
    top, rest = matrix[:PANEL], matrix[PANEL:]
    lane = lax.broadcasted_iota(jnp.int32, (PANEL, size), 1)
    sub = lax.broadcasted_iota(jnp.int32, (PANEL, size), 0)
    pivots = [jnp.broadcast_to(top[:, r : r + 1], (PANEL, size)) for r in range(PANEL)]
    top = jnp.where(lane < PANEL, jnp.where(lane == sub, 1.0, 0.0), top)
    for r in range(PANEL):
        factor = pivots[r]
        inverse = 1.0 / factor[r : r + 1]

        def reduced(value):
            scaled = value[r : r + 1] * inverse
            return jnp.where(sub == r, scaled, value - factor * scaled)

        top = reduced(top)
        for later in range(r + 1, PANEL):
            pivots[later] = reduced(pivots[later])
    column = rest
    rest = jnp.where(lane[:1] < PANEL, 0.0, rest)
    for r in range(PANEL):
        rest = rest - column[:, r : r + 1] * top[r : r + 1]
    whole = jnp.concatenate([rest, top], axis=0)
    return pltpu.roll(whole, size - PANEL, 1)


def split(value):
    high = value.astype(BF16)
    return high, (value - high.astype(F32)).astype(BF16)


def kernel(
    n, slow, fast,
    act_ref, og_ref, pin_ref, pout_ref, cin_ref, cout_ref, len_hbm, ids_hbm, bank_ref,
    out_ref, len_ref, ids_ref,
    x, proj, w, stage, bank, factor, halves, mine_buf, theirs_buf, idbuf, wide_white, wsend, wrecv, white, psend, precv,
    load_sem, gs_sem, gr_sem, relay_sem, pair_send, pair_recv, is_sem, ir_sem, ws_sem, wr_sem, ps_sem, pr_sem,
):
    group = lax.axis_index("groups")
    me = lax.axis_index("coord")
    core = me % 2
    seqs = len_ref.shape[0]
    length = x.shape[1] // seqs
    rank = cin_ref.shape[0]
    shard = pin_ref.shape[0]
    queries = out_ref.shape[1]
    per = bank_ref.shape[1] // rank
    block = wsend.shape[1]
    level = me // (2 * fast)
    forwards = core == group
    solves = core != group
    home = me // 2

    def both(first, second):
        pl.when(core == 0)(first)
        pl.when(core == 1)(second)

    def load(src, dst, at):
        return pltpu.make_async_copy(src, dst, load_sem.at[at])

    own_w = [load(pin_ref, w.at[me], 0), load(pout_ref, w.at[me], 0)]
    own_s = [load(pout_ref, stage, 1), load(pin_ref, stage, 1)]
    own_f = [load(cin_ref, factor.at[0], 2), load(cout_ref, factor.at[1], 7)]
    own_x = [load(act_ref, x.at[core], 3), load(og_ref, x.at[core], 3)]
    for pair in (own_w, own_s):
        both(pair[0].start, pair[1].start)
    own_f[0].start()
    own_f[1].start()
    len_load, ids_load = load(len_hbm, len_ref, 4), load(ids_hbm, ids_ref, 5)
    bank_load = load(bank_ref, bank, 6)
    len_load.start()
    ids_load.start()

    fasts = [2 * b for b in range(1, fast)]
    ranks = range(1, slow)
    early = ranks[:EARLY]
    twin = (1 - group, me)
    chip = 2 * fast
    near = [xor(me, chip * a) for a in range(slow)]
    inner = jnp.minimum(level, 1) * jnp.minimum(slow - 1 - level, 1)
    if slow == 4:
        near[2:] = [near[2] + inner * (near[3] - near[2]), near[3] + inner * (near[2] - near[3])]

    def slot(rank_at, off):
        return xor(near[rank_at], off)

    def peer(mask):
        return (group, xor(me, mask))

    barrier = pltpu.get_barrier_semaphore()

    def signal(semaphore, to):
        pl.semaphore_signal(semaphore, inc=1, device_id=to, device_id_type=MESH)

    below, above = (group, me - 2 * fast), (group, me + 2 * fast)
    has_below, has_above = level > 0, level < slow - 1
    pl.when(has_below)(lambda: signal(barrier, below))
    pl.when(has_above)(lambda: signal(barrier, above))
    signal(barrier, twin)
    for mask in fasts + [1]:
        signal(barrier, peer(mask))
    both(own_x[0].start, own_x[1].start)
    bank_load.start()

    own_w[0].wait()
    own_s[0].wait()
    pl.semaphore_wait(barrier, 1 + fast + jnp.minimum(level, 1) + jnp.minimum(slow - 1 - level, 1))

    piece = shard // PARTS
    count = [0]
    all_sends, forward_sends = [], []

    def shard_copy(place, part, to, at, src=None):
        rows = pl.ds(part * piece, piece)
        return pltpu.make_async_remote_copy(
            src_ref=w.at[place, rows] if src is None else src.at[rows], dst_ref=w.at[place, rows],
            send_sem=gs_sem.at[at], recv_sem=gr_sem.at[place, part],
            device_id=to, device_id_type=MESH,
        )

    def send(source, part, to, sink, src=None):
        at = count[0]

        def make():
            device = (1 - group if to[0] else group, slot(to[1], to[2]))
            return shard_copy(slot(*source), part, device, at, src)

        count[0] += 1
        make().start()
        sink.append(make)

    def arrived(rank_at, off, parts=range(PARTS)):
        for part in parts:
            shard_copy(slot(rank_at, off), part, peer(1), 0).wait_recv()

    def pair_copy(src, dst, at):
        return pltpu.make_async_remote_copy(
            src_ref=src, dst_ref=dst, send_sem=pair_send.at[at], recv_sem=pair_recv.at[at],
            device_id=peer(1), device_id_type=MESH,
        )

    def along(rank_at, sources, which):
        group_of = []

        @pl.when(which)
        def _():
            for source in sources:
                for part in range(PARTS):
                    send((0, source), part, (0, rank_at, 0), group_of)

        forward_sends.append((which, group_of))

    def relay(step):
        @pl.when(forwards)
        def _():
            pl.when(has_below)(lambda: signal(relay_sem.at[step, 0], below))
            pl.when(has_above)(lambda: signal(relay_sem.at[step, 1], above))

    def relayed(step):
        @pl.when(forwards)
        def _():
            pl.when(has_above)(lambda: pl.semaphore_wait(relay_sem.at[step, 0], 1))
            pl.when(has_below)(lambda: pl.semaphore_wait(relay_sem.at[step, 1], 1))

    for part in range(PARTS):
        send((0, 0), part, (0, 0, 1), all_sends, stage)
    if slow > 2:
        relay(1)
    middle = jnp.logical_and(forwards, inner == 1)
    outer = jnp.logical_and(forwards, inner == 0)
    special = slow == 4
    if slow > 1:
        along(1, [0], forwards)
    if special:
        along(2, [0], middle)
    for part in range(PARTS):
        for mask in fasts:
            send((0, 0), part, (0, 0, mask), all_sends)
    x_pair = [pair_copy(og_ref, x.at[core], 0), pair_copy(act_ref, x.at[core], 0)]
    both(x_pair[0].start, x_pair[1].start)
    own_f[0].wait()
    own_f[1].wait()

    def step(_, carry):
        first, second = factor[0], factor[1]
        factor[0] = eliminate_panel(first)
        factor[1] = eliminate_panel(second)
        return carry

    if slow > 2:
        relayed(1)
        if slow > 3:
            relay(2)
    if special:
        along(3, [0], middle)
        along(2, [0], outer)
    arrived(0, 1)
    if slow > 1:
        along(1, [1], forwards)
    if special:
        along(2, [1], middle)
    for part in range(PARTS):
        for mask in fasts:
            send((0, 1), part, (0, 0, mask), all_sends)
    for at in range(1, slow - 1):
        if at > 1:
            relayed(at)
            if at + 1 < slow - 1:
                relay(at + 1)
        if not special:
            along(at + 1, [0, 1], forwards)
        elif at == 1:
            along(3, [1], middle)
            along(2, [1], outer)
        else:
            along(3, [0, 1], outer)

    len_load.wait()
    ids_load.wait()
    for s in range(seqs):
        idbuf[home, core, s : s + 1] = jnp.full((1, idbuf.shape[3]), ids_ref[s], jnp.int32)
    if psend.shape[2] > queries:
        psend[...] = jnp.zeros_like(psend)
    if block > 2 * seqs * per:
        wide_white[...] = jnp.zeros_like(wide_white)

    @pl.when(solves)
    def _():
        for at in range(2):
            factor[at] = start_factor(factor[at])
        lax.fori_loop(0, rank // PANEL, step, 0)
        for at in range(2):
            high, low = split(factor[at])
            halves[at, 0] = high
            halves[at, 1] = low

    own_ids = pair_copy(idbuf.at[home, core], idbuf.at[home, core], 1)
    own_ids.start()

    def id_copy(place, at, to):
        return pltpu.make_async_remote_copy(
            src_ref=idbuf.at[place], dst_ref=idbuf.at[place],
            send_sem=is_sem.at[at], recv_sem=ir_sem.at[place],
            device_id=(group, to), device_id_type=MESH,
        )

    def from_near():
        for b in fasts:
            for c in range(2):
                arrived(0, b + c)

    def from_slow(rank_at):
        for c in range(2):
            for part in range(PARTS):
                arrived(rank_at, c, [part])
                group_of = []

                @pl.when(forwards)
                def _():
                    source = (rank_at, c)
                    for b in fasts:
                        send(source, part, (0, 0, b), group_of)
                    send(source, part, (1, 0, 0), group_of)
                    if rank_at not in early:
                        for b in fasts:
                            send(source, part, (1, 0, b), group_of)

                forward_sends.append((forwards, group_of))

    def from_fast(rank_at):
        for b in fasts:
            for c in range(2):
                for part in range(PARTS):
                    arrived(rank_at, b + c, [part])
                    if rank_at in early:
                        group_of = []

                        @pl.when(forwards)
                        def _():
                            send((rank_at, b + c), part, (1, 0, 0), group_of)

                        forward_sends.append((forwards, group_of))

    span = n // slow * shard

    def add(first, slots, shards, columns):
        value = jnp.dot(
            x[:, :, columns].reshape(2 * seqs * length, -1), w[shards].reshape(slots * shard, rank),
            preferred_element_type=F32,
        ).reshape(2, seqs * length, rank)
        if first:
            proj[...] = value
        else:
            proj[...] += value

    def load_x():
        own_x[0].wait()
        x_pair[0].wait_recv()

    def project(rank_at):
        at = near[rank_at] // chip
        add(rank_at == 0, chip, pl.ds(at * chip, chip), pl.ds(pl.multiple_of(at * span, 128), span))

    def project_pair(rank_at, off):
        at = slot(rank_at, off) // 2
        add(False, 2, pl.ds(at * 2, 2), pl.ds(pl.multiple_of(at * 2 * shard, 128), 2 * shard))

    pairs = (2 * shard) % 128 == 0 and slow > 1
    last = slow - 1

    def on_solver(event, *args):
        pl.when(solves)(functools.partial(event, *args))

    if slow == 1 or len(early) < slow - 1:
        from_near()
    for at in ranks:
        from_slow(at)
        if at == 1 and len(early) == slow - 1:
            from_near()
        if at == 1:
            load_x()
        else:
            from_fast(at - 1)
        if at < slow - 1:
            project(at - 1)
        else:
            on_solver(project, at - 1)
    if slow > 1:
        if pairs:
            on_solver(project_pair, last, 0)
        from_fast(last)
    else:
        load_x()

    @pl.when(forwards)
    def _():
        for at in range(max(0, slow - 2), slow):
            project(at)

    @pl.when(solves)
    def _():
        if pairs:
            for b in fasts:
                project_pair(last, b)
        else:
            project(last)

    position = lax.broadcasted_iota(jnp.int32, (length, 1), 0)

    def masked():
        for s in range(seqs):
            rows = slice(s * length, (s + 1) * length)
            valid = (position < len_ref[s]).astype(F32)
            proj[core, rows] = proj[core, rows] * valid
        return proj[...].astype(BF16)

    def white_at(place, j, to):
        return pltpu.make_async_remote_copy(
            src_ref=wsend.at[to], dst_ref=wrecv.at[place],
            send_sem=ws_sem.at[j], recv_sem=wr_sem.at[place],
            device_id=(group, to), device_id_type=MESH,
        )

    def white_copy(j):
        return white_at(home, j, xor(me, j))

    def swap():
        return pair_copy(mine_buf, theirs_buf, 2)

    @pl.when(forwards)
    def _():
        mine_buf[...] = masked()
        swap().start()
        own_ids.wait_recv()
        for j in range(2, n):
            id_copy(home, j, xor(me, j)).start()


    @pl.when(solves)
    def _():
        mine = masked()
        swap().wait_recv()
        theirs = theirs_buf[...]
        x_proj = jnp.where(core == 0, mine, theirs)
        d_proj = jnp.where(core == 0, theirs, mine)
        grads = []
        for s in range(2 * seqs):
            rows = slice(s % seqs * length, (s % seqs + 1) * length)
            grads.append(
                lax.dot_general(
                    d_proj[s // seqs, rows], x_proj[s // seqs, rows], (((0,), (0,)), ((), ())),
                    preferred_element_type=F32,
                )
            )
        high, low = split(jnp.concatenate(grads, axis=1))
        left = jnp.dot(
            jnp.concatenate([halves[1, 0], halves[1, 0], halves[1, 1]], axis=1),
            jnp.concatenate([high, low, high], axis=0),
            preferred_element_type=F32,
        )
        high, low = split(jnp.concatenate([left[:, s * rank : (s + 1) * rank] for s in range(2 * seqs)], axis=0))
        whites = jnp.dot(
            jnp.concatenate([high, low, high], axis=1),
            jnp.concatenate([halves[0, 0], halves[0, 0], halves[0, 1]], axis=0),
            preferred_element_type=F32,
        ).reshape(2 * seqs, n, per, rank)
        if per % 8 == 0 and block == 2 * seqs * per:
            wsend[...] = jnp.concatenate([whites[s] for s in range(2 * seqs)], axis=1).astype(BF16)
        else:
            for s in range(2 * seqs):
                wide_white[:, s * per : (s + 1) * per] = whites[s]
            wsend[...] = wide_white[...].astype(BF16)
        for j in range(n - 1, 0, -1):
            white_copy(j).start()
        wrecv[home] = wsend[me]

    def exchange(src, dst, send_sem, recv_sem, j):
        copy = pltpu.make_async_remote_copy(
            src_ref=src, dst_ref=dst,
            send_sem=send_sem.at[j], recv_sem=recv_sem.at[j],
            device_id=peer(j), device_id_type=MESH,
        )
        copy.start()
        return copy

    bank_load.wait()

    def white_arrived(place):
        white_at(place, 0, me).wait_recv()

    pl.when(forwards)(lambda: white_arrived(home))
    for j in range(1, n // 2):
        white_arrived(xor(home, j))
    white[...] = wrecv[...].astype(F32).reshape(n // 2 * block, rank)

    columns = jnp.concatenate(
        [
            jnp.concatenate(
                [white[pl.ds(s * per + a, n // 2, stride=block), :] for s in range(2 * seqs)], axis=0
            ).astype(BF16)
            for a in range(per)
        ],
        axis=1,
    )

    def partial(target):
        rows = bank[pl.ds(pl.multiple_of(target * queries, queries), queries)]
        return lax.dot_general(columns, rows, (((1,), (1,)), ((), ())), preferred_element_type=F32)

    score_copies = []
    for j in range(n - 1, 0, -1):
        psend[j, :, :queries] = partial(xor(me, j)).astype(BF16)
        score_copies.append(exchange(psend.at[j], precv.at[j], ps_sem, pr_sem, j))
    total = partial(me)
    pl.when(solves)(lambda: own_ids.wait_recv())
    for j in range(1, n // 2):
        id_copy(xor(home, j), 0, me).wait_recv()
    ids = jnp.concatenate([idbuf[:, s // seqs, s % seqs, :] for s in range(2 * seqs)], axis=0)[:, :1]
    held = n * seqs
    one_hot = (ids == lax.broadcasted_iota(jnp.int32, (held, held), 1)).astype(BF16)
    for make in all_sends:
        make().wait_send()

    def drain(makes):
        for make in makes:
            make().wait_send()

    for which, makes in forward_sends:
        pl.when(which)(functools.partial(drain, makes))
    x_pair[0].wait_send()
    pl.when(forwards)(lambda: swap().wait_send())

    @pl.when(solves)
    def _():
        for j in range(1, n):
            white_copy(j).wait_send()

    own_ids.wait_send()

    @pl.when(forwards)
    def _():
        for j in range(2, n):
            id_copy(home, j, xor(me, j)).wait_send()

    for j, copy in zip(range(n - 1, 0, -1), score_copies):
        copy.wait_recv()
        total += precv[j, :, :queries].astype(F32)
    placed = lax.dot_general(
        one_hot, total.astype(BF16), (((0,), (0,)), ((), ())), preferred_element_type=F32
    )
    out_ref[...] = placed.astype(BF16)
    for copy in score_copies:
        copy.wait_send()


def solution(mesh):
    n = mesh.shape["coord"]
    assert mesh.shape["groups"] == 2
    chips = n // 2
    slow = 1
    while slow * slow < chips:
        slow *= 2
    fast = chips // slow

    def body(activations, out_grads, proj_in, proj_out, cov_in, cov_out, lengths, seq_ids, bank):
        seqs, length, width = activations.shape
        shard, rank = proj_in.shape
        per = bank.shape[1] // rank
        queries = bank.shape[0] // n
        wide = -(-queries // 128) * 128
        block = -(-(2 * seqs * per) // 16) * 16
        held = n * seqs
        sends = 2 * (1 + fast) + 4 * slow + 2 * (slow - 1) * 2 * fast + 2 * slow * fast
        vmem = pl.BlockSpec(memory_space=pltpu.VMEM)
        hbm = pl.BlockSpec(memory_space=pltpu.HBM)
        dma = pltpu.SemaphoreType.DMA
        return pl.pallas_call(
            functools.partial(kernel, n, slow, fast),
            out_shape=jax.ShapeDtypeStruct((held, queries), BF16),
            in_specs=[hbm] * 9,
            out_specs=vmem,
            scratch_shapes=[
                pltpu.SMEM((seqs,), jnp.int32),
                pltpu.SMEM((seqs,), jnp.int32),
                pltpu.VMEM((2, seqs * length, width), BF16),
                pltpu.VMEM((2, seqs * length, rank), F32),
                pltpu.VMEM((n, shard, rank), BF16),
                pltpu.VMEM((shard, rank), BF16),
                pltpu.VMEM(bank.shape, BF16),
                pltpu.VMEM((2, rank, rank), F32),
                pltpu.VMEM((2, 2, rank, rank), BF16),
                pltpu.VMEM((2, seqs * length, rank), BF16),
                pltpu.VMEM((2, seqs * length, rank), BF16),
                pltpu.VMEM((n // 2, 2, seqs, 128), jnp.int32),
                pltpu.VMEM((n, block, rank), F32),
                pltpu.VMEM((n, block, rank), BF16),
                pltpu.VMEM((n // 2, block, rank), BF16),
                pltpu.VMEM((n // 2 * block, rank), F32),
                pltpu.VMEM((n, held, wide), BF16),
                pltpu.VMEM((n, held, wide), BF16),
                dma((8,)),
                dma((sends * PARTS,)), dma((n, PARTS)), pltpu.SemaphoreType.REGULAR((max(slow, 2), 2)),
                dma((3,)), dma((3,)), dma((n,)), dma((n // 2,)),
                dma((n,)), dma((n,)), dma((n,)), dma((n,)),
            ],
            compiler_params=pltpu.CompilerParams(
                collective_id=0, has_side_effects=True, vmem_limit_bytes=48 * 2**20
            ),
        )(*(
            pltpu.with_memory_space_constraint(array, pltpu.HBM)
            for array in (
                activations.reshape(seqs * length, width), out_grads.reshape(seqs * length, width),
                proj_in, proj_out, cov_in, cov_out, lengths, seq_ids, bank,
            )
        ))

    in_specs = (
        P(("groups", "coord"), None, None),
        P(("groups", "coord"), None, None),
        P("coord", None),
        P("coord", None),
        P(),
        P(),
        P(("groups", "coord")),
        P(("groups", "coord")),
        P(None, "coord"),
    )
    return jax.shard_map(body, mesh=mesh, in_specs=in_specs, out_specs=P("groups", "coord"), check_vma=False)
```

```python
import functools

import jax
import jax.numpy as jnp
from jax import lax
from jax.experimental import pallas as pl
from jax.experimental.pallas import tpu as pltpu
from jax.sharding import PartitionSpec as P

MESH = pl.DeviceIdType.MESH
F32 = jnp.float32
BF16 = jnp.bfloat16
PANEL = 8
PARTS = 1
EARLY = 3


def xor(value, mask):
    bit = 1
    result = value
    while bit <= mask:
        if mask & bit:
            result = result + bit - 2 * bit * ((value // bit) % 2)
        bit *= 2
    return result


def start_factor(cov):
    size = cov.shape[0]
    rows = lax.broadcasted_iota(jnp.int32, (size, size), 0)
    lanes = lax.broadcasted_iota(jnp.int32, (size, size), 1)
    diagonal = jnp.where(rows == lanes, cov, 0.0)
    damping = 0.1 * jnp.sum(diagonal) / size
    return jnp.where(rows == lanes, cov + damping, cov)


def eliminate_panel(matrix):
    size = matrix.shape[0]
    top, rest = matrix[:PANEL], matrix[PANEL:]
    lane = lax.broadcasted_iota(jnp.int32, (PANEL, size), 1)
    sub = lax.broadcasted_iota(jnp.int32, (PANEL, size), 0)
    pivots = [jnp.broadcast_to(top[:, r : r + 1], (PANEL, size)) for r in range(PANEL)]
    top = jnp.where(lane < PANEL, jnp.where(lane == sub, 1.0, 0.0), top)
    for r in range(PANEL):
        factor = pivots[r]
        inverse = 1.0 / factor[r : r + 1]

        def reduced(value):
            scaled = value[r : r + 1] * inverse
            return jnp.where(sub == r, scaled, value - factor * scaled)

        top = reduced(top)
        for later in range(r + 1, PANEL):
            pivots[later] = reduced(pivots[later])
    column = rest
    rest = jnp.where(lane[:1] < PANEL, 0.0, rest)
    for r in range(PANEL):
        rest = rest - column[:, r : r + 1] * top[r : r + 1]
    whole = jnp.concatenate([rest, top], axis=0)
    return pltpu.roll(whole, size - PANEL, 1)


def split(value):
    high = value.astype(BF16)
    return high, (value - high.astype(F32)).astype(BF16)


def kernel(
    n, slow, fast,
    act_ref, og_ref, pin_ref, pout_ref, cin_ref, cout_ref, len_hbm, ids_hbm, bank_ref,
    out_ref, len_ref, ids_ref,
    x, proj, w, stage, bank, factor, halves, mine_buf, theirs_buf, idbuf, wide_white, wsend, wrecv, white, psend, precv,
    load_sem, gs_sem, gr_sem, relay_sem, pair_send, pair_recv, is_sem, ir_sem, ws_sem, wr_sem, ps_sem, pr_sem,
):
    group = lax.axis_index("groups")
    me = lax.axis_index("coord")
    core = me % 2
    seqs = len_ref.shape[0]
    length = x.shape[1] // seqs
    rank = cin_ref.shape[0]
    shard = pin_ref.shape[0]
    queries = out_ref.shape[1]
    per = bank_ref.shape[1] // rank
    block = wsend.shape[1]
    level = me // (2 * fast)
    forwards = core == group
    solves = core != group
    home = me // 2

    def both(first, second):
        pl.when(core == 0)(first)
        pl.when(core == 1)(second)

    def load(src, dst, at):
        return pltpu.make_async_copy(src, dst, load_sem.at[at])

    own_w = [load(pin_ref, w.at[me], 0), load(pout_ref, w.at[me], 0)]
    own_s = [load(pout_ref, stage, 1), load(pin_ref, stage, 1)]
    own_f = [load(cin_ref, factor.at[0], 2), load(cout_ref, factor.at[1], 7)]
    own_x = [load(act_ref, x.at[core], 3), load(og_ref, x.at[core], 3)]
    for pair in (own_w, own_s):
        both(pair[0].start, pair[1].start)
    own_f[0].start()
    own_f[1].start()
    len_load, ids_load = load(len_hbm, len_ref, 4), load(ids_hbm, ids_ref, 5)
    bank_load = load(bank_ref, bank, 6)
    len_load.start()
    ids_load.start()

    fasts = [2 * b for b in range(1, fast)]
    ranks = range(1, slow)
    early = ranks[:EARLY]
    twin = (1 - group, me)
    chip = 2 * fast
    near = [xor(me, chip * a) for a in range(slow)]
    inner = jnp.minimum(level, 1) * jnp.minimum(slow - 1 - level, 1)
    if slow == 4:
        near[2:] = [near[2] + inner * (near[3] - near[2]), near[3] + inner * (near[2] - near[3])]

    def slot(rank_at, off):
        return xor(near[rank_at], off)

    def peer(mask):
        return (group, xor(me, mask))

    barrier = pltpu.get_barrier_semaphore()

    def signal(semaphore, to):
        pl.semaphore_signal(semaphore, inc=1, device_id=to, device_id_type=MESH)

    below, above = (group, me - 2 * fast), (group, me + 2 * fast)
    has_below, has_above = level > 0, level < slow - 1
    pl.when(has_below)(lambda: signal(barrier, below))
    pl.when(has_above)(lambda: signal(barrier, above))
    signal(barrier, twin)
    for mask in fasts + [1]:
        signal(barrier, peer(mask))
    both(own_x[0].start, own_x[1].start)
    bank_load.start()

    own_w[0].wait()
    own_s[0].wait()
    pl.semaphore_wait(barrier, 1 + fast + jnp.minimum(level, 1) + jnp.minimum(slow - 1 - level, 1))

    piece = shard // PARTS
    count = [0]
    all_sends, forward_sends = [], []

    def shard_copy(place, part, to, at, src=None):
        rows = pl.ds(part * piece, piece)
        return pltpu.make_async_remote_copy(
            src_ref=w.at[place, rows] if src is None else src.at[rows], dst_ref=w.at[place, rows],
            send_sem=gs_sem.at[at], recv_sem=gr_sem.at[place, part],
            device_id=to, device_id_type=MESH,
        )

    def send(source, part, to, sink, src=None):
        at = count[0]

        def make():
            device = (1 - group if to[0] else group, slot(to[1], to[2]))
            return shard_copy(slot(*source), part, device, at, src)

        count[0] += 1
        make().start()
        sink.append(make)

    def arrived(rank_at, off, parts=range(PARTS)):
        for part in parts:
            shard_copy(slot(rank_at, off), part, peer(1), 0).wait_recv()

    def pair_copy(src, dst, at):
        return pltpu.make_async_remote_copy(
            src_ref=src, dst_ref=dst, send_sem=pair_send.at[at], recv_sem=pair_recv.at[at],
            device_id=peer(1), device_id_type=MESH,
        )

    def along(rank_at, sources, which):
        group_of = []

        @pl.when(which)
        def _():
            for source in sources:
                for part in range(PARTS):
                    send((0, source), part, (0, rank_at, 0), group_of)

        forward_sends.append((which, group_of))

    def relay(step):
        @pl.when(forwards)
        def _():
            pl.when(has_below)(lambda: signal(relay_sem.at[step, 0], below))
            pl.when(has_above)(lambda: signal(relay_sem.at[step, 1], above))

    def relayed(step):
        @pl.when(forwards)
        def _():
            pl.when(has_above)(lambda: pl.semaphore_wait(relay_sem.at[step, 0], 1))
            pl.when(has_below)(lambda: pl.semaphore_wait(relay_sem.at[step, 1], 1))

    for part in range(PARTS):
        send((0, 0), part, (0, 0, 1), all_sends, stage)
    if slow > 2:
        relay(1)
    middle = jnp.logical_and(forwards, inner == 1)
    outer = jnp.logical_and(forwards, inner == 0)
    special = slow == 4
    if slow > 1:
        along(1, [0], forwards)
    if special:
        along(2, [0], middle)
    for part in range(PARTS):
        for mask in fasts:
            send((0, 0), part, (0, 0, mask), all_sends)
    x_pair = [pair_copy(og_ref, x.at[core], 0), pair_copy(act_ref, x.at[core], 0)]
    both(x_pair[0].start, x_pair[1].start)
    own_f[0].wait()
    own_f[1].wait()

    def step(_, carry):
        first, second = factor[0], factor[1]
        factor[0] = eliminate_panel(first)
        factor[1] = eliminate_panel(second)
        return carry

    if slow > 2:
        relayed(1)
        if slow > 3:
            relay(2)
    if special:
        along(3, [0], middle)
        along(2, [0], outer)
    arrived(0, 1)
    if slow > 1:
        along(1, [1], forwards)
    if special:
        along(2, [1], middle)
    for part in range(PARTS):
        for mask in fasts:
            send((0, 1), part, (0, 0, mask), all_sends)
    for at in range(1, slow - 1):
        if at > 1:
            relayed(at)
            if at + 1 < slow - 1:
                relay(at + 1)
        if not special:
            along(at + 1, [0, 1], forwards)
        elif at == 1:
            along(3, [1], middle)
            along(2, [1], outer)
        else:
            along(3, [0, 1], outer)

    len_load.wait()
    ids_load.wait()
    for s in range(seqs):
        idbuf[home, core, s : s + 1] = jnp.full((1, idbuf.shape[3]), ids_ref[s], jnp.int32)
    if psend.shape[2] > queries:
        psend[...] = jnp.zeros_like(psend)
    if block > 2 * seqs * per:
        wide_white[...] = jnp.zeros_like(wide_white)

    @pl.when(solves)
    def _():
        for at in range(2):
            factor[at] = start_factor(factor[at])
        lax.fori_loop(0, rank // PANEL, step, 0)
        for at in range(2):
            high, low = split(factor[at])
            halves[at, 0] = high
            halves[at, 1] = low

    own_ids = pair_copy(idbuf.at[home, core], idbuf.at[home, core], 1)
    own_ids.start()

    def id_copy(place, at, to):
        return pltpu.make_async_remote_copy(
            src_ref=idbuf.at[place], dst_ref=idbuf.at[place],
            send_sem=is_sem.at[at], recv_sem=ir_sem.at[place],
            device_id=(group, to), device_id_type=MESH,
        )

    def from_near():
        for b in fasts:
            for c in range(2):
                arrived(0, b + c)

    def from_slow(rank_at):
        for c in range(2):
            for part in range(PARTS):
                arrived(rank_at, c, [part])
                group_of = []

                @pl.when(forwards)
                def _():
                    source = (rank_at, c)
                    for b in fasts:
                        send(source, part, (0, 0, b), group_of)
                    send(source, part, (1, 0, 0), group_of)
                    if rank_at not in early:
                        for b in fasts:
                            send(source, part, (1, 0, b), group_of)

                forward_sends.append((forwards, group_of))

    def from_fast(rank_at):
        for b in fasts:
            for c in range(2):
                for part in range(PARTS):
                    arrived(rank_at, b + c, [part])
                    if rank_at in early:
                        group_of = []

                        @pl.when(forwards)
                        def _():
                            send((rank_at, b + c), part, (1, 0, 0), group_of)

                        forward_sends.append((forwards, group_of))

    span = n // slow * shard

    def add(first, slots, shards, columns):
        value = jnp.dot(
            x[:, :, columns].reshape(2 * seqs * length, -1), w[shards].reshape(slots * shard, rank),
            preferred_element_type=F32,
        ).reshape(2, seqs * length, rank)
        if first:
            proj[...] = value
        else:
            proj[...] += value

    def load_x():
        own_x[0].wait()
        x_pair[0].wait_recv()

    def project(rank_at):
        at = near[rank_at] // chip
        add(rank_at == 0, chip, pl.ds(at * chip, chip), pl.ds(pl.multiple_of(at * span, 128), span))

    def project_pair(rank_at, off):
        at = slot(rank_at, off) // 2
        add(False, 2, pl.ds(at * 2, 2), pl.ds(pl.multiple_of(at * 2 * shard, 128), 2 * shard))

    pairs = (2 * shard) % 128 == 0 and slow > 1
    last = slow - 1

    def on_solver(event, *args):
        pl.when(solves)(functools.partial(event, *args))

    if slow == 1 or len(early) < slow - 1:
        from_near()
    for at in ranks:
        from_slow(at)
        if at == 1 and len(early) == slow - 1:
            from_near()
        if at == 1:
            load_x()
        else:
            from_fast(at - 1)
        if at < slow - 1:
            project(at - 1)
        else:
            on_solver(project, at - 1)
    if slow > 1:
        if pairs:
            on_solver(project_pair, last, 0)
        from_fast(last)
    else:
        load_x()

    @pl.when(forwards)
    def _():
        for at in range(max(0, slow - 2), slow):
            project(at)

    @pl.when(solves)
    def _():
        if pairs:
            for b in fasts:
                project_pair(last, b)
        else:
            project(last)

    position = lax.broadcasted_iota(jnp.int32, (length, 1), 0)

    def masked():
        for s in range(seqs):
            rows = slice(s * length, (s + 1) * length)
            valid = (position < len_ref[s]).astype(F32)
            proj[core, rows] = proj[core, rows] * valid
        return proj[...].astype(BF16)

    def white_at(place, j, to):
        return pltpu.make_async_remote_copy(
            src_ref=wsend.at[to], dst_ref=wrecv.at[place],
            send_sem=ws_sem.at[j], recv_sem=wr_sem.at[place],
            device_id=(group, to), device_id_type=MESH,
        )

    def white_copy(j):
        return white_at(home, j, xor(me, j))

    def swap():
        return pair_copy(mine_buf, theirs_buf, 2)

    @pl.when(forwards)
    def _():
        mine_buf[...] = masked()
        swap().start()
        own_ids.wait_recv()
        for j in range(2, n):
            id_copy(home, j, xor(me, j)).start()


    @pl.when(solves)
    def _():
        mine = masked()
        swap().wait_recv()
        theirs = theirs_buf[...]
        x_proj = jnp.where(core == 0, mine, theirs)
        d_proj = jnp.where(core == 0, theirs, mine)
        grads = []
        for s in range(2 * seqs):
            rows = slice(s % seqs * length, (s % seqs + 1) * length)
            grads.append(
                lax.dot_general(
                    d_proj[s // seqs, rows], x_proj[s // seqs, rows], (((0,), (0,)), ((), ())),
                    preferred_element_type=F32,
                )
            )
        high, low = split(jnp.concatenate(grads, axis=1))
        stacked = jnp.concatenate([high, low, high], axis=0)
        inner_in = jnp.concatenate([halves[0, 0], halves[0, 0], halves[0, 1]], axis=0)
        for far in (1, 0):
            side = xor(me // (n // 2), far)
            rows = pl.ds(pl.multiple_of(side * (rank // 2), 16), rank // 2)
            targets = pl.ds(side * (n // 2), n // 2)
            left = jnp.dot(
                jnp.concatenate([halves[1, 0, rows], halves[1, 0, rows], halves[1, 1, rows]], axis=1),
                stacked,
                preferred_element_type=F32,
            )
            high, low = split(jnp.concatenate([left[:, s * rank : (s + 1) * rank] for s in range(2 * seqs)], axis=0))
            whites = jnp.dot(
                jnp.concatenate([high, low, high], axis=1), inner_in, preferred_element_type=F32
            ).reshape(2 * seqs, n // 2, per, rank)
            if per % 8 == 0 and block == 2 * seqs * per:
                wsend[targets] = jnp.concatenate([whites[s] for s in range(2 * seqs)], axis=1).astype(BF16)
            else:
                for s in range(2 * seqs):
                    wide_white[targets, s * per : (s + 1) * per] = whites[s]
                wsend[targets] = wide_white[targets].astype(BF16)
            for j in range(n - 1, n // 2 - 1, -1) if far else range(n // 2 - 1, 0, -1):
                white_copy(j).start()
        wrecv[home] = wsend[me]

    def exchange(src, dst, send_sem, recv_sem, j):
        copy = pltpu.make_async_remote_copy(
            src_ref=src, dst_ref=dst,
            send_sem=send_sem.at[j], recv_sem=recv_sem.at[j],
            device_id=peer(j), device_id_type=MESH,
        )
        copy.start()
        return copy

    bank_load.wait()

    def white_arrived(place):
        white_at(place, 0, me).wait_recv()

    pl.when(forwards)(lambda: white_arrived(home))
    for j in range(1, n // 2):
        white_arrived(xor(home, j))
    white[...] = wrecv[...].astype(F32).reshape(n // 2 * block, rank)

    columns = jnp.concatenate(
        [
            jnp.concatenate(
                [white[pl.ds(s * per + a, n // 2, stride=block), :] for s in range(2 * seqs)], axis=0
            ).astype(BF16)
            for a in range(per)
        ],
        axis=1,
    )

    def partial(target):
        rows = bank[pl.ds(pl.multiple_of(target * queries, queries), queries)]
        return lax.dot_general(columns, rows, (((1,), (1,)), ((), ())), preferred_element_type=F32)

    score_copies = []
    for j in range(n - 1, 0, -1):
        psend[j, :, :queries] = partial(xor(me, j)).astype(BF16)
        score_copies.append(exchange(psend.at[j], precv.at[j], ps_sem, pr_sem, j))
    total = partial(me)
    pl.when(solves)(lambda: own_ids.wait_recv())
    for j in range(1, n // 2):
        id_copy(xor(home, j), 0, me).wait_recv()
    ids = jnp.concatenate([idbuf[:, s // seqs, s % seqs, :] for s in range(2 * seqs)], axis=0)[:, :1]
    held = n * seqs
    one_hot = (ids == lax.broadcasted_iota(jnp.int32, (held, held), 1)).astype(BF16)
    for make in all_sends:
        make().wait_send()

    def drain(makes):
        for make in makes:
            make().wait_send()

    for which, makes in forward_sends:
        pl.when(which)(functools.partial(drain, makes))
    x_pair[0].wait_send()
    pl.when(forwards)(lambda: swap().wait_send())

    @pl.when(solves)
    def _():
        for j in range(1, n):
            white_copy(j).wait_send()

    own_ids.wait_send()

    @pl.when(forwards)
    def _():
        for j in range(2, n):
            id_copy(home, j, xor(me, j)).wait_send()

    for j, copy in zip(range(n - 1, 0, -1), score_copies):
        copy.wait_recv()
        total += precv[j, :, :queries].astype(F32)
    placed = lax.dot_general(
        one_hot, total.astype(BF16), (((0,), (0,)), ((), ())), preferred_element_type=F32
    )
    out_ref[...] = placed.astype(BF16)
    for copy in score_copies:
        copy.wait_send()


def solution(mesh):
    n = mesh.shape["coord"]
    assert mesh.shape["groups"] == 2
    chips = n // 2
    slow = 1
    while slow * slow < chips:
        slow *= 2
    fast = chips // slow

    def body(activations, out_grads, proj_in, proj_out, cov_in, cov_out, lengths, seq_ids, bank):
        seqs, length, width = activations.shape
        shard, rank = proj_in.shape
        per = bank.shape[1] // rank
        queries = bank.shape[0] // n
        wide = -(-queries // 128) * 128
        block = -(-(2 * seqs * per) // 16) * 16
        held = n * seqs
        sends = 2 * (1 + fast) + 4 * slow + 2 * (slow - 1) * 2 * fast + 2 * slow * fast
        vmem = pl.BlockSpec(memory_space=pltpu.VMEM)
        hbm = pl.BlockSpec(memory_space=pltpu.HBM)
        dma = pltpu.SemaphoreType.DMA
        return pl.pallas_call(
            functools.partial(kernel, n, slow, fast),
            out_shape=jax.ShapeDtypeStruct((held, queries), BF16),
            in_specs=[hbm] * 9,
            out_specs=vmem,
            scratch_shapes=[
                pltpu.SMEM((seqs,), jnp.int32),
                pltpu.SMEM((seqs,), jnp.int32),
                pltpu.VMEM((2, seqs * length, width), BF16),
                pltpu.VMEM((2, seqs * length, rank), F32),
                pltpu.VMEM((n, shard, rank), BF16),
                pltpu.VMEM((shard, rank), BF16),
                pltpu.VMEM(bank.shape, BF16),
                pltpu.VMEM((2, rank, rank), F32),
                pltpu.VMEM((2, 2, rank, rank), BF16),
                pltpu.VMEM((2, seqs * length, rank), BF16),
                pltpu.VMEM((2, seqs * length, rank), BF16),
                pltpu.VMEM((n // 2, 2, seqs, 128), jnp.int32),
                pltpu.VMEM((n, block, rank), F32),
                pltpu.VMEM((n, block, rank), BF16),
                pltpu.VMEM((n // 2, block, rank), BF16),
                pltpu.VMEM((n // 2 * block, rank), F32),
                pltpu.VMEM((n, held, wide), BF16),
                pltpu.VMEM((n, held, wide), BF16),
                dma((8,)),
                dma((sends * PARTS,)), dma((n, PARTS)), pltpu.SemaphoreType.REGULAR((max(slow, 2), 2)),
                dma((3,)), dma((3,)), dma((n,)), dma((n // 2,)),
                dma((n,)), dma((n,)), dma((n,)), dma((n,)),
            ],
            compiler_params=pltpu.CompilerParams(
                collective_id=0, has_side_effects=True, vmem_limit_bytes=48 * 2**20
            ),
        )(*(
            pltpu.with_memory_space_constraint(array, pltpu.HBM)
            for array in (
                activations.reshape(seqs * length, width), out_grads.reshape(seqs * length, width),
                proj_in, proj_out, cov_in, cov_out, lengths, seq_ids, bank,
            )
        ))

    in_specs = (
        P(("groups", "coord"), None, None),
        P(("groups", "coord"), None, None),
        P("coord", None),
        P("coord", None),
        P(),
        P(),
        P(("groups", "coord")),
        P(("groups", "coord")),
        P(None, "coord"),
    )
    return jax.shard_map(body, mesh=mesh, in_specs=in_specs, out_specs=P("groups", "coord"), check_vma=False)
```

```python
import functools

import jax
import jax.numpy as jnp
from jax import lax
from jax.experimental import pallas as pl
from jax.experimental.pallas import tpu as pltpu
from jax.sharding import PartitionSpec as P

MESH = pl.DeviceIdType.MESH
F32 = jnp.float32
BF16 = jnp.bfloat16
PANEL = 8
PARTS = 1
EARLY = 3


def xor(value, mask):
    bit = 1
    result = value
    while bit <= mask:
        if mask & bit:
            result = result + bit - 2 * bit * ((value // bit) % 2)
        bit *= 2
    return result


def start_factor(cov):
    size = cov.shape[0]
    rows = lax.broadcasted_iota(jnp.int32, (size, size), 0)
    lanes = lax.broadcasted_iota(jnp.int32, (size, size), 1)
    diagonal = jnp.where(rows == lanes, cov, 0.0)
    damping = 0.1 * jnp.sum(diagonal) / size
    return jnp.where(rows == lanes, cov + damping, cov)


def eliminate_panel(matrix):
    size = matrix.shape[0]
    top, rest = matrix[:PANEL], matrix[PANEL:]
    lane = lax.broadcasted_iota(jnp.int32, (PANEL, size), 1)
    sub = lax.broadcasted_iota(jnp.int32, (PANEL, size), 0)
    pivots = [jnp.broadcast_to(top[:, r : r + 1], (PANEL, size)) for r in range(PANEL)]
    top = jnp.where(lane < PANEL, jnp.where(lane == sub, 1.0, 0.0), top)
    for r in range(PANEL):
        factor = pivots[r]
        inverse = 1.0 / factor[r : r + 1]

        def reduced(value):
            scaled = value[r : r + 1] * inverse
            return jnp.where(sub == r, scaled, value - factor * scaled)

        top = reduced(top)
        for later in range(r + 1, PANEL):
            pivots[later] = reduced(pivots[later])
    column = rest
    rest = jnp.where(lane[:1] < PANEL, 0.0, rest)
    for r in range(PANEL):
        rest = rest - column[:, r : r + 1] * top[r : r + 1]
    whole = jnp.concatenate([rest, top], axis=0)
    return pltpu.roll(whole, size - PANEL, 1)


def split(value):
    high = value.astype(BF16)
    return high, (value - high.astype(F32)).astype(BF16)


def kernel(
    n, slow, fast,
    act_ref, og_ref, pin_ref, pout_ref, cin_ref, cout_ref, len_hbm, ids_hbm, bank_ref,
    out_ref, len_ref, ids_ref,
    x, proj, w, stage, bank, factor, halves, mine_buf, theirs_buf, idbuf, wide_white, wsend, wrecv, white, psend, precv,
    load_sem, gs_sem, gr_sem, relay_sem, pair_send, pair_recv, is_sem, ir_sem, ws_sem, wr_sem, ps_sem, pr_sem,
):
    group = lax.axis_index("groups")
    me = lax.axis_index("coord")
    core = me % 2
    seqs = len_ref.shape[0]
    length = x.shape[1] // seqs
    rank = cin_ref.shape[0]
    shard = pin_ref.shape[0]
    queries = out_ref.shape[1]
    per = bank_ref.shape[1] // rank
    block = wsend.shape[1]
    level = me // (2 * fast)
    forwards = core == group
    solves = core != group
    home = me // 2

    def both(first, second):
        pl.when(core == 0)(first)
        pl.when(core == 1)(second)

    def load(src, dst, at):
        return pltpu.make_async_copy(src, dst, load_sem.at[at])

    own_w = [load(pin_ref, w.at[me], 0), load(pout_ref, w.at[me], 0)]
    own_s = [load(pout_ref, stage, 1), load(pin_ref, stage, 1)]
    own_f = [load(cin_ref, factor.at[0], 2), load(cout_ref, factor.at[1], 7)]
    own_x = [load(act_ref, x.at[core], 3), load(og_ref, x.at[core], 3)]
    fasts = [2 * b for b in range(1, fast)]
    ranks = range(1, slow)
    early = ranks[:EARLY]
    twin = (1 - group, me)
    chip = 2 * fast
    near = [xor(me, chip * a) for a in range(slow)]
    inner = jnp.minimum(level, 1) * jnp.minimum(slow - 1 - level, 1)
    if slow == 4:
        near[2:] = [near[2] + inner * (near[3] - near[2]), near[3] + inner * (near[2] - near[3])]

    def slot(rank_at, off):
        return xor(near[rank_at], off)

    def peer(mask):
        return (group, xor(me, mask))

    barrier = pltpu.get_barrier_semaphore()

    def signal(semaphore, to):
        pl.semaphore_signal(semaphore, inc=1, device_id=to, device_id_type=MESH)

    below, above = (group, me - 2 * fast), (group, me + 2 * fast)
    has_below, has_above = level > 0, level < slow - 1
    pl.when(has_below)(lambda: signal(barrier, below))
    pl.when(has_above)(lambda: signal(barrier, above))
    signal(barrier, twin)
    for mask in fasts + [1]:
        signal(barrier, peer(mask))
    for pair in (own_w, own_s):
        both(pair[0].start, pair[1].start)
    own_f[0].start()
    own_f[1].start()
    len_load, ids_load = load(len_hbm, len_ref, 4), load(ids_hbm, ids_ref, 5)
    bank_load = load(bank_ref, bank, 6)
    len_load.start()
    ids_load.start()

    own_w[0].wait()
    own_s[0].wait()
    pl.semaphore_wait(barrier, 1 + fast + jnp.minimum(level, 1) + jnp.minimum(slow - 1 - level, 1))

    piece = shard // PARTS
    count = [0]
    all_sends, forward_sends = [], []

    def shard_copy(place, part, to, at, src=None):
        rows = pl.ds(part * piece, piece)
        return pltpu.make_async_remote_copy(
            src_ref=w.at[place, rows] if src is None else src.at[rows], dst_ref=w.at[place, rows],
            send_sem=gs_sem.at[at], recv_sem=gr_sem.at[place, part],
            device_id=to, device_id_type=MESH,
        )

    def send(source, part, to, sink, src=None):
        at = count[0]

        def make():
            device = (1 - group if to[0] else group, slot(to[1], to[2]))
            return shard_copy(slot(*source), part, device, at, src)

        count[0] += 1
        make().start()
        sink.append(make)

    def arrived(rank_at, off, parts=range(PARTS)):
        for part in parts:
            shard_copy(slot(rank_at, off), part, peer(1), 0).wait_recv()

    def pair_copy(src, dst, at):
        return pltpu.make_async_remote_copy(
            src_ref=src, dst_ref=dst, send_sem=pair_send.at[at], recv_sem=pair_recv.at[at],
            device_id=peer(1), device_id_type=MESH,
        )

    def along(rank_at, sources, which):
        group_of = []

        @pl.when(which)
        def _():
            for source in sources:
                for part in range(PARTS):
                    send((0, source), part, (0, rank_at, 0), group_of)

        forward_sends.append((which, group_of))

    def relay(step):
        @pl.when(forwards)
        def _():
            pl.when(has_below)(lambda: signal(relay_sem.at[step, 0], below))
            pl.when(has_above)(lambda: signal(relay_sem.at[step, 1], above))

    def relayed(step):
        @pl.when(forwards)
        def _():
            pl.when(has_above)(lambda: pl.semaphore_wait(relay_sem.at[step, 0], 1))
            pl.when(has_below)(lambda: pl.semaphore_wait(relay_sem.at[step, 1], 1))

    for part in range(PARTS):
        send((0, 0), part, (0, 0, 1), all_sends, stage)
    if slow > 2:
        relay(1)
    middle = jnp.logical_and(forwards, inner == 1)
    outer = jnp.logical_and(forwards, inner == 0)
    special = slow == 4
    if slow > 1:
        along(1, [0], forwards)
    if special:
        along(2, [0], middle)
    for part in range(PARTS):
        for mask in fasts:
            send((0, 0), part, (0, 0, mask), all_sends)
    both(own_x[0].start, own_x[1].start)
    bank_load.start()
    x_pair = [pair_copy(og_ref, x.at[core], 0), pair_copy(act_ref, x.at[core], 0)]
    both(x_pair[0].start, x_pair[1].start)
    own_f[0].wait()
    own_f[1].wait()

    def step(_, carry):
        first, second = factor[0], factor[1]
        factor[0] = eliminate_panel(first)
        factor[1] = eliminate_panel(second)
        return carry

    if slow > 2:
        relayed(1)
        if slow > 3:
            relay(2)
    if special:
        along(3, [0], middle)
        along(2, [0], outer)
    arrived(0, 1)
    if slow > 1:
        along(1, [1], forwards)
    if special:
        along(2, [1], middle)
    for part in range(PARTS):
        for mask in fasts:
            send((0, 1), part, (0, 0, mask), all_sends)
    for at in range(1, slow - 1):
        if at > 1:
            relayed(at)
            if at + 1 < slow - 1:
                relay(at + 1)
        if not special:
            along(at + 1, [0, 1], forwards)
        elif at == 1:
            along(3, [1], middle)
            along(2, [1], outer)
        else:
            along(3, [0, 1], outer)

    len_load.wait()
    ids_load.wait()
    for s in range(seqs):
        idbuf[home, core, s : s + 1] = jnp.full((1, idbuf.shape[3]), ids_ref[s], jnp.int32)
    if psend.shape[2] > queries:
        psend[...] = jnp.zeros_like(psend)
    if block > 2 * seqs * per:
        wide_white[...] = jnp.zeros_like(wide_white)

    @pl.when(solves)
    def _():
        for at in range(2):
            factor[at] = start_factor(factor[at])
        lax.fori_loop(0, rank // PANEL, step, 0)
        for at in range(2):
            high, low = split(factor[at])
            halves[at, 0] = high
            halves[at, 1] = low

    own_ids = pair_copy(idbuf.at[home, core], idbuf.at[home, core], 1)
    own_ids.start()

    def id_copy(place, at, to):
        return pltpu.make_async_remote_copy(
            src_ref=idbuf.at[place], dst_ref=idbuf.at[place],
            send_sem=is_sem.at[at], recv_sem=ir_sem.at[place],
            device_id=(group, to), device_id_type=MESH,
        )

    def from_near():
        for b in fasts:
            for c in range(2):
                arrived(0, b + c)

    def from_slow(rank_at):
        for c in range(2):
            for part in range(PARTS):
                arrived(rank_at, c, [part])
                group_of = []

                @pl.when(forwards)
                def _():
                    source = (rank_at, c)
                    for b in fasts:
                        send(source, part, (0, 0, b), group_of)
                    send(source, part, (1, 0, 0), group_of)
                    if rank_at not in early:
                        for b in fasts:
                            send(source, part, (1, 0, b), group_of)

                forward_sends.append((forwards, group_of))

    def from_fast(rank_at):
        for b in fasts:
            for c in range(2):
                for part in range(PARTS):
                    arrived(rank_at, b + c, [part])
                    if rank_at in early:
                        group_of = []

                        @pl.when(forwards)
                        def _():
                            send((rank_at, b + c), part, (1, 0, 0), group_of)

                        forward_sends.append((forwards, group_of))

    span = n // slow * shard

    def add(first, slots, shards, columns):
        value = jnp.dot(
            x[:, :, columns].reshape(2 * seqs * length, -1), w[shards].reshape(slots * shard, rank),
            preferred_element_type=F32,
        ).reshape(2, seqs * length, rank)
        if first:
            proj[...] = value
        else:
            proj[...] += value

    def load_x():
        own_x[0].wait()
        x_pair[0].wait_recv()

    def project(rank_at):
        at = near[rank_at] // chip
        add(rank_at == 0, chip, pl.ds(at * chip, chip), pl.ds(pl.multiple_of(at * span, 128), span))

    def project_pair(rank_at, off):
        at = slot(rank_at, off) // 2
        add(False, 2, pl.ds(at * 2, 2), pl.ds(pl.multiple_of(at * 2 * shard, 128), 2 * shard))

    pairs = (2 * shard) % 128 == 0 and slow > 1
    last = slow - 1

    def on_solver(event, *args):
        pl.when(solves)(functools.partial(event, *args))

    if slow == 1 or len(early) < slow - 1:
        from_near()
    for at in ranks:
        from_slow(at)
        if at == 1 and len(early) == slow - 1:
            from_near()
        if at == 1:
            load_x()
        else:
            from_fast(at - 1)
        if at < slow - 1:
            project(at - 1)
        else:
            on_solver(project, at - 1)
    if slow > 1:
        if pairs:
            on_solver(project_pair, last, 0)
        from_fast(last)
    else:
        load_x()

    @pl.when(forwards)
    def _():
        for at in range(max(0, slow - 2), slow):
            project(at)

    @pl.when(solves)
    def _():
        if pairs:
            for b in fasts:
                project_pair(last, b)
        else:
            project(last)

    position = lax.broadcasted_iota(jnp.int32, (length, 1), 0)

    def masked():
        for s in range(seqs):
            rows = slice(s * length, (s + 1) * length)
            valid = (position < len_ref[s]).astype(F32)
            proj[core, rows] = proj[core, rows] * valid
        return proj[...].astype(BF16)

    def white_at(place, j, to):
        return pltpu.make_async_remote_copy(
            src_ref=wsend.at[to], dst_ref=wrecv.at[place],
            send_sem=ws_sem.at[j], recv_sem=wr_sem.at[place],
            device_id=(group, to), device_id_type=MESH,
        )

    def white_copy(j):
        return white_at(home, j, xor(me, j))

    def swap():
        return pair_copy(mine_buf, theirs_buf, 2)

    @pl.when(forwards)
    def _():
        mine_buf[...] = masked()
        swap().start()
        own_ids.wait_recv()
        for j in range(2, n):
            id_copy(home, j, xor(me, j)).start()


    @pl.when(solves)
    def _():
        mine = masked()
        swap().wait_recv()
        theirs = theirs_buf[...]
        x_proj = jnp.where(core == 0, mine, theirs)
        d_proj = jnp.where(core == 0, theirs, mine)
        grads = []
        for s in range(2 * seqs):
            rows = slice(s % seqs * length, (s % seqs + 1) * length)
            grads.append(
                lax.dot_general(
                    d_proj[s // seqs, rows], x_proj[s // seqs, rows], (((0,), (0,)), ((), ())),
                    preferred_element_type=F32,
                )
            )
        high, low = split(jnp.concatenate(grads, axis=1))
        stacked = jnp.concatenate([high, low, high], axis=0)
        inner_in = jnp.concatenate([halves[0, 0], halves[0, 0], halves[0, 1]], axis=0)
        for far in (1, 0):
            side = xor(me // (n // 2), far)
            rows = pl.ds(pl.multiple_of(side * (rank // 2), 16), rank // 2)
            targets = pl.ds(side * (n // 2), n // 2)
            left = jnp.dot(
                jnp.concatenate([halves[1, 0, rows], halves[1, 0, rows], halves[1, 1, rows]], axis=1),
                stacked,
                preferred_element_type=F32,
            )
            high, low = split(jnp.concatenate([left[:, s * rank : (s + 1) * rank] for s in range(2 * seqs)], axis=0))
            whites = jnp.dot(
                jnp.concatenate([high, low, high], axis=1), inner_in, preferred_element_type=F32
            ).reshape(2 * seqs, n // 2, per, rank)
            if per % 8 == 0 and block == 2 * seqs * per:
                wsend[targets] = jnp.concatenate([whites[s] for s in range(2 * seqs)], axis=1).astype(BF16)
            else:
                for s in range(2 * seqs):
                    wide_white[targets, s * per : (s + 1) * per] = whites[s]
                wsend[targets] = wide_white[targets].astype(BF16)
            for j in range(n - 1, n // 2 - 1, -1) if far else range(n // 2 - 1, 0, -1):
                white_copy(j).start()
        wrecv[home] = wsend[me]

    def exchange(src, dst, send_sem, recv_sem, j):
        copy = pltpu.make_async_remote_copy(
            src_ref=src, dst_ref=dst,
            send_sem=send_sem.at[j], recv_sem=recv_sem.at[j],
            device_id=peer(j), device_id_type=MESH,
        )
        copy.start()
        return copy

    bank_load.wait()

    def white_arrived(place):
        white_at(place, 0, me).wait_recv()

    def widen(place):
        white[pl.ds(pl.multiple_of(place * block, block), block)] = wrecv[place].astype(F32)

    pl.when(forwards)(lambda: white_arrived(home))
    widen(home)
    for j in range(1, n // 2):
        white_arrived(xor(home, j))
        widen(xor(home, j))

    columns = jnp.concatenate(
        [
            jnp.concatenate(
                [white[pl.ds(s * per + a, n // 2, stride=block), :] for s in range(2 * seqs)], axis=0
            ).astype(BF16)
            for a in range(per)
        ],
        axis=1,
    )

    def partial(target):
        rows = bank[pl.ds(pl.multiple_of(target * queries, queries), queries)]
        return lax.dot_general(columns, rows, (((1,), (1,)), ((), ())), preferred_element_type=F32)

    score_copies = []
    for j in range(n - 1, 0, -1):
        psend[j, :, :queries] = partial(xor(me, j)).astype(BF16)
        score_copies.append(exchange(psend.at[j], precv.at[j], ps_sem, pr_sem, j))
    total = partial(me)
    pl.when(solves)(lambda: own_ids.wait_recv())
    for j in range(1, n // 2):
        id_copy(xor(home, j), 0, me).wait_recv()
    ids = jnp.concatenate([idbuf[:, s // seqs, s % seqs, :] for s in range(2 * seqs)], axis=0)[:, :1]
    held = n * seqs
    one_hot = (ids == lax.broadcasted_iota(jnp.int32, (held, held), 1)).astype(BF16)
    for make in all_sends:
        make().wait_send()

    def drain(makes):
        for make in makes:
            make().wait_send()

    for which, makes in forward_sends:
        pl.when(which)(functools.partial(drain, makes))
    x_pair[0].wait_send()
    pl.when(forwards)(lambda: swap().wait_send())

    @pl.when(solves)
    def _():
        for j in range(1, n):
            white_copy(j).wait_send()

    own_ids.wait_send()

    @pl.when(forwards)
    def _():
        for j in range(2, n):
            id_copy(home, j, xor(me, j)).wait_send()

    for j, copy in zip(range(n - 1, 0, -1), score_copies):
        copy.wait_recv()
        total += precv[j, :, :queries].astype(F32)
    placed = lax.dot_general(
        one_hot, total.astype(BF16), (((0,), (0,)), ((), ())), preferred_element_type=F32
    )
    out_ref[...] = placed.astype(BF16)
    for copy in score_copies:
        copy.wait_send()


def solution(mesh):
    n = mesh.shape["coord"]
    assert mesh.shape["groups"] == 2
    chips = n // 2
    slow = 1
    while slow * slow < chips:
        slow *= 2
    fast = chips // slow

    def body(activations, out_grads, proj_in, proj_out, cov_in, cov_out, lengths, seq_ids, bank):
        seqs, length, width = activations.shape
        shard, rank = proj_in.shape
        per = bank.shape[1] // rank
        queries = bank.shape[0] // n
        wide = -(-queries // 128) * 128
        block = -(-(2 * seqs * per) // 16) * 16
        held = n * seqs
        sends = 2 * (1 + fast) + 4 * slow + 2 * (slow - 1) * 2 * fast + 2 * slow * fast
        vmem = pl.BlockSpec(memory_space=pltpu.VMEM)
        hbm = pl.BlockSpec(memory_space=pltpu.HBM)
        dma = pltpu.SemaphoreType.DMA
        return pl.pallas_call(
            functools.partial(kernel, n, slow, fast),
            out_shape=jax.ShapeDtypeStruct((held, queries), BF16),
            in_specs=[hbm] * 9,
            out_specs=vmem,
            scratch_shapes=[
                pltpu.SMEM((seqs,), jnp.int32),
                pltpu.SMEM((seqs,), jnp.int32),
                pltpu.VMEM((2, seqs * length, width), BF16),
                pltpu.VMEM((2, seqs * length, rank), F32),
                pltpu.VMEM((n, shard, rank), BF16),
                pltpu.VMEM((shard, rank), BF16),
                pltpu.VMEM(bank.shape, BF16),
                pltpu.VMEM((2, rank, rank), F32),
                pltpu.VMEM((2, 2, rank, rank), BF16),
                pltpu.VMEM((2, seqs * length, rank), BF16),
                pltpu.VMEM((2, seqs * length, rank), BF16),
                pltpu.VMEM((n // 2, 2, seqs, 128), jnp.int32),
                pltpu.VMEM((n, block, rank), F32),
                pltpu.VMEM((n, block, rank), BF16),
                pltpu.VMEM((n // 2, block, rank), BF16),
                pltpu.VMEM((n // 2 * block, rank), F32),
                pltpu.VMEM((n, held, wide), BF16),
                pltpu.VMEM((n, held, wide), BF16),
                dma((8,)),
                dma((sends * PARTS,)), dma((n, PARTS)), pltpu.SemaphoreType.REGULAR((max(slow, 2), 2)),
                dma((3,)), dma((3,)), dma((n,)), dma((n // 2,)),
                dma((n,)), dma((n,)), dma((n,)), dma((n,)),
            ],
            compiler_params=pltpu.CompilerParams(
                collective_id=0, has_side_effects=True, vmem_limit_bytes=48 * 2**20
            ),
        )(*(
            pltpu.with_memory_space_constraint(array, pltpu.HBM)
            for array in (
                activations.reshape(seqs * length, width), out_grads.reshape(seqs * length, width),
                proj_in, proj_out, cov_in, cov_out, lengths, seq_ids, bank,
            )
        ))

    in_specs = (
        P(("groups", "coord"), None, None),
        P(("groups", "coord"), None, None),
        P("coord", None),
        P("coord", None),
        P(),
        P(),
        P(("groups", "coord")),
        P(("groups", "coord")),
        P(None, "coord"),
    )
    return jax.shard_map(body, mesh=mesh, in_specs=in_specs, out_specs=P("groups", "coord"), check_vma=False)
```
